32 devices in a mesh: groups: 2 (over x), scene: 16 (over z, y, core).
Axes of the slice: x: 2, y: 2, z: 4, core: 2. Of those that a mesh axis runs over, the one named last changes fastest.
Arguments:
- tokens: bfloat16 [32, 196, 768], P(('groups', 'scene')), parts along dimension 0, may hold values from -6 to 6
- qkv_weight: bfloat16 [768, 2304], replicated, may hold values from -0.21875 to 0.21875
- out_weight: bfloat16 [768, 768], replicated, may hold values from -0.21875 to 0.21875
- attn_gain: float32 [768], replicated, may hold values from 0.1 to 1.9
- head_gain: float32 [768], replicated, may hold values from 0.1 to 1.9
- head_weight: bfloat16 [768, 1024], replicated, may hold values from -0.21875 to 0.21875
- head_bias: float32 [1024], replicated, may hold values from -3 to 3
- pair_list: int32 [64, 2], P('groups'), parts along dimension 0, may hold values from 0 to 15, as said below
- pair_count: int32 [32], P('groups'), parts along dimension 0, may hold values from 1 to 2, as said below
Outputs:
- joined: float32 [32, 196, 768], P(('groups', 'scene')), parts along dimension 0
The draws below stay inside these ranges and needn't reach their ends.
There are 2 independent parts, one for each index of `groups`. The reference program is written for one: setup_inputs(seed, part) draws one part's arguments, and reference() takes and returns one part's arrays. A program takes and returns all parts, laid end to end along the dimension named above; an argument that names none is the same for every part. Nothing has to cross between parts.
Inputs may be any that keep to these rules, and one draw needn't show every extreme that they name: `pair_list`: slot j of device d (row d * 2 + j) holds a pair whose first image is d + (j mod 1); its second image is owned by a device 1 to 2 places away along the scene axis taken as a cycle, image i being owned by device i. `pair_count`: entry d is the number of live slots of device d; slots from that number on are ignored. In every draw some device has exactly 2 and another exactly 1.
All inputs are finite; a program needn't handle non-finite values.
Results may differ from the reference program's by a relative error of at most 0.0045.
Values may be sent and summed in bfloat16 or wider, within the bound.
No kernel may reach another device: no remote copies, remote signals or barrier semaphores. Data moves between devices by JAX's collectives and lax.ppermute only.
A program may use at most 128 MiB of HBM per device.

```python
import jax
import jax.numpy as jnp
from jax import lax

D = 768
HEADS = 12
TOK = 196
PM = 1024
IMG_DEV = 1
PAIR_DEV = 2
REACH = 2
IMAGES = 16
PAIRS = 32


def draw_pair_list(key, part):
    slot_index = jnp.arange(PAIRS, dtype=jnp.int32)
    device = slot_index // PAIR_DEV
    first_image = device * IMG_DEV + slot_index % PAIR_DEV % IMG_DEV
    key_a, key_b, key_c = jax.random.split(jax.random.fold_in(key, 11), 3)
    distance = jax.random.randint(key_a, (PAIRS,), 1, REACH + 1, dtype=jnp.int32)
    direction = jax.random.randint(key_b, (PAIRS,), 0, 2, dtype=jnp.int32) * 2 - 1
    member = jax.random.randint(key_c, (PAIRS,), 0, IMG_DEV, dtype=jnp.int32)
    devices = PAIRS // PAIR_DEV
    other_device = (device + direction * distance) % devices
    second_image = other_device * IMG_DEV + member
    return jnp.stack([first_image, second_image], axis=1).astype(jnp.int32)


def draw_pair_count(key, part):
    devices = PAIRS // PAIR_DEV
    key_a, key_b, key_c, key_d = jax.random.split(jax.random.fold_in(key, 23), 4)
    first_draw = jax.random.randint(key_a, (devices,), IMG_DEV, PAIR_DEV + 1, dtype=jnp.int32)
    second_draw = jax.random.randint(key_d, (devices,), IMG_DEV, PAIR_DEV + 1, dtype=jnp.int32)
    counts = jnp.minimum(first_draw, second_draw)
    highest = jax.random.randint(key_b, (), 0, devices, dtype=jnp.int32)
    lowest = (highest + 1 + jax.random.randint(key_c, (), 0, devices - 1, dtype=jnp.int32)) % devices
    positions = jnp.arange(devices, dtype=jnp.int32)
    counts = jnp.where(positions == highest, PAIR_DEV, counts)
    counts = jnp.where(positions == lowest, IMG_DEV, counts)
    return counts.astype(jnp.int32)


def block_scale(own_key, dims, cuts, low, high):
    gain, own = 1.0, jax.random.fold_in(own_key, 6)
    for axis_at, parts in cuts:
        steps = jnp.exp(jax.random.uniform(jax.random.fold_in(own, axis_at), (parts,), jnp.float32, low / len(cuts), high / len(cuts)))
        gain = gain * jnp.repeat(steps, dims[axis_at] // parts).reshape([-1 if axis == axis_at else 1 for axis in range(len(dims))])
    return gain


def noise(rng, extent, scale, limit, cuts=(), kind=jnp.bfloat16):
    array = jax.random.normal(rng, extent, jnp.float32) * scale
    if len(cuts) > 0:
        array = block_scale(rng, extent, cuts, -0.22, 0.18) * array
    return jnp.clip(array, min=-limit, max=limit).astype(kind)


def setup_inputs(seed: int = 0, part: int = 0) -> dict:
    key_list = jax.random.split(jax.random.key(seed), 10)
    part_splits = jax.random.split(jax.random.fold_in(key_list[9], part), 10)
    tokens = noise(part_splits[0], (IMAGES, TOK, D), 1.0, 6.0, ((0, 16),))
    qkv_weight = noise(key_list[1], (D, 3 * D), D ** -0.5, 0.21875)
    out_weight = noise(key_list[2], (D, D), D ** -0.5, 0.21875)
    attn_gain = jnp.clip(1.0 + 0.18 * jax.random.normal(key_list[3], (D,), jnp.float32), 0.1, 1.9)
    head_gain = jnp.clip(1.0 + 0.18 * jax.random.normal(key_list[4], (D,), jnp.float32), 0.1, 1.9)
    head_weight = noise(key_list[5], (D, PM), D ** -0.5, 0.21875)
    head_bias = noise(key_list[6], (PM,), 0.5, 3.0, (), jnp.float32)
    pair_list = draw_pair_list(jax.random.fold_in(jax.random.fold_in(key_list[9], part), 71), part)
    pair_count = draw_pair_count(jax.random.fold_in(jax.random.fold_in(key_list[9], part), 71), part)
    return {"tokens": tokens, "qkv_weight": qkv_weight, "out_weight": out_weight, "attn_gain": attn_gain, "head_gain": head_gain, "head_weight": head_weight, "head_bias": head_bias, "pair_list": pair_list, "pair_count": pair_count}


TEMPER = 16.0
CONF_RANGE = 4.0
EPSILON = 1e-06

def layer_norm(values, gain_vec):
    centred = values - lax.optimization_barrier(jnp.mean(values, axis=-1, keepdims=True))
    spread = lax.optimization_barrier(jnp.mean(centred * centred, axis=-1, keepdims=True))
    return centred * lax.rsqrt(spread + EPSILON) * gain_vec

def head_unit(values):
    shaped = values.reshape(values.shape[:-1] + (HEADS, values.shape[-1] // HEADS))
    energy = lax.optimization_barrier(jnp.mean(shaped * shaped, axis=-1, keepdims=True))
    return (shaped * lax.rsqrt(energy + EPSILON)).reshape(values.shape)

def project(single_image, attn_gain, qkv_weight):
    model_width = single_image.shape[-1]
    normed = layer_norm(single_image.astype(jnp.float32), attn_gain.astype(jnp.float32)).astype(jnp.bfloat16)
    mixed = jnp.dot(normed, qkv_weight, preferred_element_type=jnp.float32)
    queries = head_unit(mixed[:, :model_width]).astype(jnp.bfloat16)
    key_rows = head_unit(mixed[:, model_width:2 * model_width]).astype(jnp.bfloat16)
    values = mixed[:, 2 * model_width:].astype(jnp.bfloat16)
    return (queries, key_rows, values)

def view_maps(own_rows, queries, key_rows, values, out_weight, head_gain, head_weight, head_bias):
    view_count, token_count, model_width = own_rows.shape
    head_size = model_width // HEADS
    query_heads = queries.astype(jnp.float32).reshape(view_count, token_count, HEADS, head_size)
    key_heads = key_rows.astype(jnp.float32).reshape(view_count, token_count, HEADS, head_size)
    value_heads = values.astype(jnp.float32).reshape(view_count, token_count, HEADS, head_size)
    scores = jnp.einsum('vthc,vshc->vhts', query_heads, key_heads) * (TEMPER / head_size)
    exponent = jnp.exp(scores)
    attention = (exponent / lax.optimization_barrier(jnp.sum(exponent, axis=-1, keepdims=True))).astype(jnp.bfloat16)
    attended = jnp.einsum('vhts,vshc->vthc', attention.astype(jnp.float32), value_heads)
    attended = attended.reshape(view_count, token_count, model_width).astype(jnp.bfloat16)
    mixed = own_rows.astype(jnp.float32) + jnp.einsum('vtd,de->vte', attended.astype(jnp.float32), out_weight.astype(jnp.float32))
    head_in = layer_norm(mixed, head_gain.astype(jnp.float32)).astype(jnp.bfloat16)
    head_out = jnp.einsum('vtd,de->vte', head_in.astype(jnp.float32), head_weight.astype(jnp.float32)) + head_bias.astype(jnp.float32)
    xyz_cols = 3 * (head_weight.shape[1] // 4)
    return (head_out[..., :xyz_cols].astype(jnp.bfloat16), head_out[..., xyz_cols:].astype(jnp.bfloat16))

def reference(tokens, qkv_weight, out_weight, attn_gain, head_gain, head_weight, head_bias, pair_list, pair_count):
    all_queries, all_keys, all_values = lax.map(lambda single_image: project(single_image, attn_gain, qkv_weight), tokens)
    pixels = head_weight.shape[1] // 4
    image_count, token_count, model_width = tokens.shape

    def add_pair(totals, slot_index):
        weighted_sum, weight_sum = totals
        pair_rows = pair_list[slot_index]
        partner_ids = pair_rows[::-1]
        device = slot_index // PAIR_DEV
        live_flag = (slot_index % PAIR_DEV < pair_count[device]).astype(jnp.float32)
        xyz, conf = view_maps(tokens[pair_rows], all_queries[pair_rows], all_keys[partner_ids], all_values[partner_ids], out_weight, head_gain, head_weight, head_bias)
        weight = jnp.exp(CONF_RANGE * jnp.tanh(conf.astype(jnp.float32) / CONF_RANGE)) * live_flag
        weighted = (weight[:, :, None, :] * xyz.astype(jnp.float32).reshape(2, token_count, 3, pixels)).reshape(2, token_count, 3 * pixels)
        weighted_sum = weighted_sum.at[pair_rows].add(weighted)
        weight_sum = weight_sum.at[pair_rows].add(weight)
        return ((weighted_sum, weight_sum), None)
    start = (jnp.zeros((image_count, token_count, 3 * pixels), jnp.float32), jnp.zeros((image_count, token_count, pixels), jnp.float32))
    (weighted_sum, weight_sum), _ = lax.scan(add_pair, start, jnp.arange(pair_list.shape[0], dtype=jnp.int32))
    return weighted_sum / jnp.tile(weight_sum, (1, 1, 3))
```

```python
import functools

import jax
import jax.numpy as jnp
from jax import lax
from jax.experimental import pallas as pl
from jax.experimental.pallas import tpu as pltpu
from jax.sharding import PartitionSpec as P

HEADS = 12
TEMPER = 16.0
CONF_RANGE = 4.0
EPSILON = 1e-06
LANES = 128
MXU = 256

VMEM_SPEC = pl.BlockSpec(memory_space=pltpu.VMEM)
SMEM_SPEC = pl.BlockSpec(memory_space=pltpu.SMEM)


def round_up(value, step):
    return -(-value // step) * step


def layer_norm(values, gain_row):
    centred = values - jnp.mean(values, axis=-1, keepdims=True)
    spread = jnp.mean(centred * centred, axis=-1, keepdims=True)
    return centred * lax.rsqrt(spread + EPSILON) * gain_row


def matmul(left, right):
    return jnp.dot(left, right, preferred_element_type=jnp.float32)


def head_block(head_size):
    rows = lax.broadcasted_iota(jnp.int32, (MXU, MXU), 0) // head_size
    cols = lax.broadcasted_iota(jnp.int32, (MXU, MXU), 1) // head_size
    return jnp.where(rows == cols, 1.0 / head_size, 0.0).astype(jnp.bfloat16)


def head_unit(mixed, block):
    energy = matmul((mixed * mixed).astype(jnp.bfloat16), block)
    return (mixed * lax.rsqrt(energy + EPSILON)).astype(jnp.bfloat16)


def multiplicity(pair_list, pair_count, own, partner, slots):
    count = jnp.int32(0)
    for slot in range(slots):
        for first, second in ((own, partner), (partner, own)):
            live = slot < pair_count[first]
            hit = pair_list[first * slots + slot, 1] == second
            count = count + jnp.where(jnp.logical_and(live, hit), 1, 0)
    return count


def views_kernel(kinds, first, last, scene_size, slots, *refs):
    refs = list(refs)
    pair_list, pair_count, own_ref = refs[:3]
    partners = refs[3 : 3 + len(kinds)]
    refs = refs[3 + len(kinds) :]
    qkv_ref, out_ref, attn_gain_ref, head_gain_ref, head_ref, bias_ref = refs[:6]
    refs = refs[6:]
    if first:
        q_ref, sums_ref, weights_ref = refs[:3]
        refs = refs[3:]
    else:
        q_ref, sums_in, weights_in = refs[:3]
        refs = refs[3:]
        if last:
            joined_ref = refs[0]
            refs = refs[1:]
            sums_ref, weights_ref = refs[:2]
        else:
            sums_ref, weights_ref = refs[:2]
        refs = refs[2:]
    keys_scr, vals_scr, att_scr = refs
    tokens, width = own_ref.shape
    pixels = head_ref.shape[1] // 4
    head_size = width // HEADS
    rows = q_ref.shape[1] // 2
    padded = keys_scr.shape[0]
    pairs = width // LANES

    position = lax.axis_index("scene")
    parity = lax.rem(position, 2)
    step_to_mate = 1 - 2 * parity
    offsets = {"mate": step_to_mate, "left": -2, "right": 2, "cross": -step_to_mate}
    lane = lax.broadcasted_iota(jnp.int32, (1, LANES), 1)
    low_head = lane < head_size
    block = head_block(head_size)

    keys_scr[...] = jnp.zeros_like(keys_scr)
    row = lax.broadcasted_iota(jnp.int32, (padded, MXU), 0)
    col = lax.broadcasted_iota(jnp.int32, (padded, MXU), 1)
    ones = jnp.where(jnp.logical_and(row < tokens, col >= LANES), 1.0, 0.0).astype(jnp.bfloat16)
    for pair in range(pairs):
        vals_scr[pair] = ones

    if first:
        normed = layer_norm(own_ref[...].astype(jnp.float32), attn_gain_ref[...]).astype(jnp.bfloat16)
        q_ref[...] = jnp.zeros_like(q_ref)
        for start in range(0, width, MXU):
            unit = head_unit(matmul(normed, qkv_ref[:, start : start + MXU]), block)
            for half in range(MXU // LANES):
                pair = start // LANES + half
                piece = unit[:, half * LANES : (half + 1) * LANES]
                zero = jnp.zeros_like(piece)
                q_ref[pair, :tokens, :] = jnp.where(low_head, piece, zero)
                q_ref[pair, rows : rows + tokens, :] = jnp.where(low_head, zero, piece)
        sums_ref[...] = jnp.zeros_like(sums_ref)
        weights_ref[...] = jnp.zeros_like(weights_ref)
    else:
        sums_ref[...] = sums_in[...]
        weights_ref[...] = weights_in[...]

    for kind, partner_ref in zip(kinds, partners):
        partner = lax.rem(position + offsets[kind] + scene_size, scene_size)
        count = multiplicity(pair_list, pair_count, position, partner, slots)

        @pl.when(count > 0)
        def _():
            normed = layer_norm(partner_ref[...].astype(jnp.float32), attn_gain_ref[...]).astype(jnp.bfloat16)
            for start in range(0, width, MXU):
                keys_scr[:tokens, start : start + MXU] = head_unit(
                    matmul(normed, qkv_ref[:, width + start : width + start + MXU]), block
                )
                value = matmul(normed, qkv_ref[:, 2 * width + start : 2 * width + start + MXU]).astype(jnp.bfloat16)
                for half in range(MXU // LANES):
                    vals_scr[start // LANES + half, :tokens, :LANES] = value[:, half * LANES : (half + 1) * LANES]
            for pair in range(pairs):
                scores = lax.dot_general(
                    q_ref[pair],
                    keys_scr[:, pair * LANES : (pair + 1) * LANES],
                    (((1,), (1,)), ((), ())),
                    preferred_element_type=jnp.float32,
                )
                exponent = jnp.exp(scores * (TEMPER / head_size)).astype(jnp.bfloat16)
                mixed = matmul(exponent, vals_scr[pair])
                top = jnp.where(low_head, mixed[:tokens, :LANES], mixed[rows : rows + tokens, :LANES])
                norm = jnp.where(low_head, mixed[:tokens, LANES:], mixed[rows : rows + tokens, LANES:])
                att_scr[:, pair * LANES : (pair + 1) * LANES] = (top / norm).astype(jnp.bfloat16)
            mixed = own_ref[...].astype(jnp.float32) + matmul(att_scr[...], out_ref[...])
            head_in = layer_norm(mixed, head_gain_ref[...]).astype(jnp.bfloat16)
            conf = matmul(head_in, head_ref[:, 3 * pixels :]) + bias_ref[:, 3 * pixels :]
            conf = conf.astype(jnp.bfloat16).astype(jnp.float32)
            weight = jnp.exp(CONF_RANGE * jnp.tanh(conf / CONF_RANGE)) * count.astype(jnp.float32)
            weights_ref[...] += weight
            for part in range(3):
                cols = slice(part * pixels, (part + 1) * pixels)
                xyz = matmul(head_in, head_ref[:, cols]) + bias_ref[:, cols]
                sums_ref[:, cols] += weight * xyz.astype(jnp.bfloat16).astype(jnp.float32)

    if last:
        for part in range(3):
            cols = slice(part * pixels, (part + 1) * pixels)
            joined_ref[:, cols] = sums_ref[:, cols] / weights_ref[...]


def run_views(kinds, first, last, scene_size, pair_list, pair_count, own, partners, params, state):
    tokens, width = own.shape
    slots = pair_list.shape[0] // scene_size
    pixels = params[4].shape[1] // 4
    rows = round_up(tokens, 16)
    padded = round_up(tokens, MXU)
    pairs = width // LANES
    f32, bf16 = jnp.float32, jnp.bfloat16
    sums = jax.ShapeDtypeStruct((tokens, 3 * pixels), f32)
    weights = jax.ShapeDtypeStruct((tokens, pixels), f32)
    scratch = []
    if first:
        out_shape = (jax.ShapeDtypeStruct((pairs, 2 * rows, LANES), bf16), sums, weights)
    elif last:
        out_shape = jax.ShapeDtypeStruct((tokens, 3 * pixels), f32)
        scratch = [pltpu.VMEM(sums.shape, f32), pltpu.VMEM(weights.shape, f32)]
    else:
        out_shape = (sums, weights)
    scratch += [
        pltpu.VMEM((padded, width), bf16),
        pltpu.VMEM((pairs, padded, MXU), bf16),
        pltpu.VMEM((tokens, width), bf16),
    ]
    operands = [pair_list, pair_count, own, *partners, *params, *state]
    return pl.pallas_call(
        functools.partial(views_kernel, kinds, first, last, scene_size, slots),
        out_shape=out_shape,
        in_specs=[SMEM_SPEC, SMEM_SPEC] + [VMEM_SPEC] * (len(operands) - 2),
        out_specs=jax.tree.map(lambda _: VMEM_SPEC, out_shape),
        scratch_shapes=scratch,
        compiler_params=pltpu.CompilerParams(vmem_limit_bytes=24 * 2**20),
        cost_estimate=pl.CostEstimate(
            flops=len(kinds) * 4 * tokens * width * width * 2, bytes_accessed=8 * 2**20, transcendentals=0
        ),
        name="views_" + "_".join(kinds),
    )(*operands)


def per_device(
    tokens, qkv_weight, out_weight, attn_gain, head_gain, head_weight, head_bias, pair_list, pair_count
):
    scene_size = lax.axis_size("scene")
    own = tokens[0]
    params = (
        qkv_weight,
        out_weight,
        attn_gain.reshape(1, -1),
        head_gain.reshape(1, -1),
        head_weight,
        head_bias.reshape(1, -1),
    )

    def moved(value, target_of):
        return lax.ppermute(value, "scene", [(s, target_of(s)) for s in range(scene_size)])

    mate = moved(own, lambda s: s ^ 1)
    left = moved(own, lambda s: (s + 2) % scene_size)
    right = moved(own, lambda s: (s - 2) % scene_size)
    views = functools.partial(run_views, scene_size=scene_size, pair_list=pair_list, pair_count=pair_count, own=own, params=params)
    queries, sums, weights = views(("mate",), True, False, partners=(mate,), state=())
    parity = lax.rem(lax.axis_index("scene"), 2)
    cross = moved(jnp.where(parity == 0, right, left), lambda s: s ^ 1)
    sums, weights = views(("left", "right"), False, False, partners=(left, right), state=(queries, sums, weights))
    joined = views(("cross",), False, True, partners=(cross,), state=(queries, sums, weights))
    return joined[None]


def solution(mesh):
    return jax.shard_map(
        per_device,
        mesh=mesh,
        in_specs=(
            P(("groups", "scene"), None, None),
            P(),
            P(),
            P(),
            P(),
            P(),
            P(),
            P("groups", None),
            P("groups"),
        ),
        out_specs=P(("groups", "scene"), None, None),
        check_vma=False,
    )
```

```python
import functools

import jax
import jax.numpy as jnp
from jax import lax
from jax.experimental import pallas as pl
from jax.experimental.pallas import tpu as pltpu
from jax.sharding import PartitionSpec as P


HEADS = 12
TEMPER = 16.0
CONF_RANGE = 4.0
EPSILON = 1e-06
LANES = 128
MXU = 256

VMEM_SPEC = pl.BlockSpec(memory_space=pltpu.VMEM)
HBM_SPEC = pl.BlockSpec(memory_space=pltpu.HBM)


def in_hbm(value):
    return pltpu.with_memory_space_constraint(value, pltpu.HBM)


def round_up(value, step):
    return -(-value // step) * step


def layer_norm(values, gain_row):
    centred = values - jnp.mean(values, axis=-1, keepdims=True)
    spread = jnp.mean(centred * centred, axis=-1, keepdims=True)
    return centred * lax.rsqrt(spread + EPSILON) * gain_row


def matmul(left, right):
    return jnp.dot(left, right, preferred_element_type=jnp.float32)


def head_block(head_size):
    rows = lax.broadcasted_iota(jnp.int32, (MXU, MXU), 0) // head_size
    cols = lax.broadcasted_iota(jnp.int32, (MXU, MXU), 1) // head_size
    return jnp.where(rows == cols, 1.0 / head_size, 0.0).astype(jnp.bfloat16)


def head_unit(mixed, block):
    energy = matmul((mixed * mixed).astype(jnp.bfloat16), block)
    return (mixed * lax.rsqrt(energy + EPSILON)).astype(jnp.bfloat16)


def multiplicity(pair_list, pair_count, own, partner, slots):
    count = jnp.int32(0)
    for slot in range(slots):
        for first, second in ((own, partner), (partner, own)):
            live = slot < pair_count[first]
            hit = pair_list[1, first * slots + slot] == second
            count = count + jnp.where(jnp.logical_and(live, hit), 1, 0)
    return count


def one_view(partner, count_row, own_ref, q_ref, kv_ref, out_ref, head_ref, gains_ref, bias_ref, keys_scr, vals_scr, att_scr, emit):
    tokens, width = own_ref.shape
    head_size = width // HEADS
    pixels = head_ref.shape[1] // 4
    rows = q_ref.shape[1] // 2
    padded = keys_scr.shape[0]
    pairs = width // LANES
    low_head = lax.broadcasted_iota(jnp.int32, (1, LANES), 1) < head_size
    block = head_block(head_size)

    tail = tokens // 16 * 16
    keys_scr[tail:, :] = jnp.zeros((padded - tail, width), jnp.bfloat16)
    row = lax.broadcasted_iota(jnp.int32, (padded, LANES), 0)
    ones = jnp.where(row < tokens, 1.0, 0.0).astype(jnp.bfloat16)
    for pair in range(pairs):
        vals_scr[pair, tail:, :LANES] = jnp.zeros((padded - tail, LANES), jnp.bfloat16)
        vals_scr[pair, :, LANES:] = ones

    normed = layer_norm(partner.astype(jnp.float32), gains_ref[0:1, :]).astype(jnp.bfloat16)
    for start in range(0, width, MXU):
        keys_scr[:tokens, start : start + MXU] = head_unit(matmul(normed, kv_ref[:, start : start + MXU]), block)
        value = matmul(normed, kv_ref[:, width + start : width + start + MXU]).astype(jnp.bfloat16)
        for half in range(MXU // LANES):
            vals_scr[start // LANES + half, :tokens, :LANES] = value[:, half * LANES : (half + 1) * LANES]
    for pair in range(pairs):
        scores = lax.dot_general(
            q_ref[pair],
            keys_scr[:, pair * LANES : (pair + 1) * LANES],
            (((1,), (1,)), ((), ())),
            preferred_element_type=jnp.float32,
        )
        exponent = jnp.exp(scores * (TEMPER / head_size)).astype(jnp.bfloat16)
        mixed = matmul(exponent, vals_scr[pair])
        top = jnp.where(low_head, mixed[:tokens, :LANES], mixed[rows : rows + tokens, :LANES])
        norm = jnp.where(low_head, mixed[:tokens, LANES:], mixed[rows : rows + tokens, LANES:])
        att_scr[:, pair * LANES : (pair + 1) * LANES] = (top / norm).astype(jnp.bfloat16)
    mixed = own_ref[...].astype(jnp.float32) + matmul(att_scr[...], out_ref[...])
    head_in = layer_norm(mixed, gains_ref[1:2, :]).astype(jnp.bfloat16)
    conf = matmul(head_in, head_ref[:, 3 * pixels :]) + bias_ref[:, 3 * pixels :]
    conf = conf.astype(jnp.bfloat16).astype(jnp.float32)
    weight = jnp.exp(CONF_RANGE * jnp.tanh(conf / CONF_RANGE)) * count_row
    for part in range(3):
        cols = slice(part * pixels, (part + 1) * pixels)
        xyz = matmul(head_in, head_ref[:, cols]) + bias_ref[:, cols]
        emit(part, cols, weight, weight * xyz.astype(jnp.bfloat16).astype(jnp.float32))


def view_scratch(tokens, width):
    padded, pairs = round_up(tokens, MXU), width // LANES
    return [
        pltpu.VMEM((padded, width), jnp.bfloat16),
        pltpu.VMEM((pairs, padded, MXU), jnp.bfloat16),
        pltpu.VMEM((tokens, width), jnp.bfloat16),
    ]


def first_kernel(
    scene_size,
    slots,
    offsets_of,
    tokens_hbm,
    qkv_hbm,
    out_hbm,
    attn_gain_hbm,
    head_gain_hbm,
    head_hbm,
    bias_hbm,
    list_hbm,
    count_hbm,
    own_ref,
    kv_ref,
    out_ref,
    head_ref,
    gains_ref,
    bias_ref,
    counts_ref,
    q_ref,
    wq_scr,
    list_smem,
    count_smem,
    sems,
):
    tokens, width = own_ref.shape
    head_size = width // HEADS
    rows = q_ref.shape[1] // 2
    plan = [
        (tokens_hbm.at[0], own_ref),
        (attn_gain_hbm, gains_ref.at[0]),
        (qkv_hbm.at[:, :width], wq_scr),
        (head_gain_hbm, gains_ref.at[1]),
        (bias_hbm, bias_ref.at[0]),
        (list_hbm, list_smem),
        (count_hbm, count_smem),
        (qkv_hbm.at[:, width : 2 * width], kv_ref.at[:, :width]),
        (qkv_hbm.at[:, 2 * width :], kv_ref.at[:, width:]),
        (out_hbm, out_ref),
        (head_hbm, head_ref),
    ]
    copies = [pltpu.make_async_copy(source, target, sems.at[at]) for at, (source, target) in enumerate(plan)]
    for copy in copies:
        copy.start()
    for copy in copies[:3]:
        copy.wait()
    low_head = lax.broadcasted_iota(jnp.int32, (1, LANES), 1) < head_size
    block = head_block(head_size)
    normed = layer_norm(own_ref[...].astype(jnp.float32), gains_ref[0:1, :]).astype(jnp.bfloat16)
    q_ref[...] = jnp.zeros_like(q_ref)
    for start in range(0, width, MXU):
        unit = head_unit(matmul(normed, wq_scr[:, start : start + MXU]), block)
        for half in range(MXU // LANES):
            pair = start // LANES + half
            piece = unit[:, half * LANES : (half + 1) * LANES]
            zero = jnp.zeros_like(piece)
            q_ref[pair, :tokens, :] = jnp.where(low_head, piece, zero)
            q_ref[pair, rows : rows + tokens, :] = jnp.where(low_head, zero, piece)
    for copy in copies[3:]:
        copy.wait()
    position = lax.axis_index("scene")
    for at, offset in enumerate(offsets_of(position)):
        partner = lax.rem(position + offset + scene_size, scene_size)
        count = multiplicity(list_smem, count_smem, position, partner, slots).astype(jnp.float32)
        counts_ref[at] = jnp.full(counts_ref.shape[1:], count, jnp.float32)


def view_kernel(
    at, first, last, own_ref, kv_ref, out_ref, head_ref, gains_ref, bias_ref, counts_ref, q_ref, partner_ref, *refs
):
    if not first:
        sums_in, weights_in, *refs = refs
    if last:
        joined_hbm, keys_scr, vals_scr, att_scr, joined_scr, sems = refs
    else:
        sums_ref, weights_ref, keys_scr, vals_scr, att_scr = refs
    copies = []

    def emit(part, cols, weight, weighted):
        total = weighted if first else sums_in[:, cols] + weighted
        weight = weight if first else weights_in[...] + weight
        if last:
            joined_scr[:, cols] = total / weight
            copy = pltpu.make_async_copy(joined_scr.at[:, cols], joined_hbm.at[:, 0, cols], sems.at[part])
            copy.start()
            copies.append(copy)
        else:
            sums_ref[:, cols] = total
            if part == 0:
                weights_ref[...] = weight

    one_view(
        partner_ref[...], counts_ref[at, 0:1, 0:1], own_ref, q_ref, kv_ref, out_ref, head_ref, gains_ref, bias_ref,
        keys_scr, vals_scr, att_scr, emit,
    )
    for copy in copies:
        copy.wait()


def per_device(
    tokens, qkv_weight, out_weight, attn_gain, head_gain, head_weight, head_bias, pair_list, pair_count
):
    scene_size = lax.axis_size("scene")
    _, token_count, width = tokens.shape
    slots = pair_list.shape[0] // scene_size
    columns = head_weight.shape[1]
    pixels = columns // 4
    f32, bf16 = jnp.float32, jnp.bfloat16
    own = tokens[0]

    def moved(value, target_of):
        return lax.ppermute(value, "scene", [(s, target_of(s) % scene_size) for s in range(scene_size)])

    def mate_of(s):
        return s ^ 1

    def offsets_of(position):
        to_mate = 1 - 2 * lax.rem(position, 2)
        return (to_mate, -to_mate, 2 * to_mate, -2 * to_mate)

    sums = jax.ShapeDtypeStruct((token_count, 3 * pixels), f32)
    weights = jax.ShapeDtypeStruct((token_count, pixels), f32)
    params = pltpu.CompilerParams(vmem_limit_bytes=24 * 2**20)
    cost = pl.CostEstimate(flops=4 * token_count * width * width * 2, bytes_accessed=2**20, transcendentals=0)

    alpha = moved(own, lambda s: s + 1 if s % 2 else s - 1)
    mate = moved(own, mate_of)
    first_shapes = (
        jax.ShapeDtypeStruct((token_count, width), bf16),
        jax.ShapeDtypeStruct((width, 2 * width), bf16),
        jax.ShapeDtypeStruct(out_weight.shape, bf16),
        jax.ShapeDtypeStruct(head_weight.shape, bf16),
        jax.ShapeDtypeStruct((2, width), f32),
        jax.ShapeDtypeStruct((1, columns), f32),
        jax.ShapeDtypeStruct((4, 8, LANES), f32),
        jax.ShapeDtypeStruct((width // LANES, 2 * round_up(token_count, 16), LANES), bf16),
    )
    state = pl.pallas_call(
        functools.partial(first_kernel, scene_size, slots, offsets_of),
        out_shape=first_shapes,
        in_specs=[HBM_SPEC] * 9,
        out_specs=tuple(VMEM_SPEC for _ in first_shapes),
        scratch_shapes=[
            pltpu.VMEM((width, width), bf16),
            pltpu.SMEM((2, pair_list.shape[0]), jnp.int32),
            pltpu.SMEM(pair_count.shape, jnp.int32),
            pltpu.SemaphoreType.DMA((11,)),
        ],
        compiler_params=params,
        cost_estimate=cost,
        name="load_queries",
    )(
        in_hbm(tokens),
        *(in_hbm(value) for value in (qkv_weight, out_weight, attn_gain, head_gain, head_weight, head_bias)),
        in_hbm(pair_list.T),
        in_hbm(pair_count),
    )

    def view(at, partner, totals, last=False):
        out_shape = jax.ShapeDtypeStruct((token_count, 1, 3 * pixels), f32) if last else (sums, weights)
        scratch = view_scratch(token_count, width)
        if last:
            scratch += [pltpu.VMEM(sums.shape, f32), pltpu.SemaphoreType.DMA((3,))]
        operands = (*state, partner, *totals)
        return pl.pallas_call(
            functools.partial(view_kernel, at, not totals, last),
            out_shape=out_shape,
            in_specs=[VMEM_SPEC] * len(operands),
            out_specs=HBM_SPEC if last else (VMEM_SPEC, VMEM_SPEC),
            scratch_shapes=scratch,
            compiler_params=params,
            cost_estimate=cost,
        )(*operands)

    own, queries = lax.optimization_barrier((own, state[-1]))
    state = (*state[:-1], queries)
    beta = moved(own, lambda s: s - 2 if s % 2 else s + 2)
    totals = view(0, mate, ())
    alpha, *totals = lax.optimization_barrier((alpha, *totals))
    swapped = moved(alpha, mate_of)
    totals = view(1, alpha, totals)
    totals = view(2, swapped, totals)
    return view(3, beta, totals, last=True).transpose(1, 0, 2)


def solution(mesh):
    return jax.shard_map(
        per_device,
        mesh=mesh,
        in_specs=(
            P(("groups", "scene"), None, None),
            P(),
            P(),
            P(),
            P(),
            P(),
            P(),
            P("groups", None),
            P("groups"),
        ),
        out_specs=P(("groups", "scene"), None, None),
        check_vma=False,
    )
```

```python
import functools

import jax
import jax.numpy as jnp
from jax import lax
from jax.experimental import pallas as pl
from jax.experimental.pallas import tpu as pltpu
from jax.sharding import PartitionSpec as P


HEADS = 12
TEMPER = 16.0
CONF_RANGE = 4.0
EPSILON = 1e-06
LANES = 128
MXU = 256

VMEM_SPEC = pl.BlockSpec(memory_space=pltpu.VMEM)
HBM_SPEC = pl.BlockSpec(memory_space=pltpu.HBM)


def in_hbm(value):
    return pltpu.with_memory_space_constraint(value, pltpu.HBM)


def round_up(value, step):
    return -(-value // step) * step


def layer_norm(values, gain_row):
    centred = values - jnp.mean(values, axis=-1, keepdims=True)
    spread = jnp.mean(centred * centred, axis=-1, keepdims=True)
    return centred * lax.rsqrt(spread + EPSILON) * gain_row


def matmul(left, right):
    return jnp.dot(left, right, preferred_element_type=jnp.float32)


def head_block(head_size):
    rows = lax.broadcasted_iota(jnp.int32, (MXU, MXU), 0) // head_size
    cols = lax.broadcasted_iota(jnp.int32, (MXU, MXU), 1) // head_size
    return jnp.where(rows == cols, 1.0 / head_size, 0.0).astype(jnp.bfloat16)


def head_unit(mixed, block):
    energy = matmul((mixed * mixed).astype(jnp.bfloat16), block)
    return (mixed * lax.rsqrt(energy + EPSILON)).astype(jnp.bfloat16)


def multiplicity(pair_list, pair_count, own, partner, slots):
    count = jnp.int32(0)
    for slot in range(slots):
        for first, second in ((own, partner), (partner, own)):
            live = slot < pair_count[first]
            hit = pair_list[1, first * slots + slot] == second
            count = count + jnp.where(jnp.logical_and(live, hit), 1, 0)
    return count


def one_view(partner, count_row, own_ref, q_ref, qkv_ref, out_ref, head_ref, gains_ref, bias_ref, keys_scr, vals_scr, att_scr, loads, emit):
    tokens, width = own_ref.shape
    head_size = width // HEADS
    pixels = head_ref.shape[1] // 4
    rows = q_ref.shape[1] // 2
    padded = keys_scr.shape[0]
    pairs = width // LANES
    low_head = lax.broadcasted_iota(jnp.int32, (1, LANES), 1) < head_size
    block = head_block(head_size)

    tail = tokens // 16 * 16
    keys_scr[tail:, :] = jnp.zeros((padded - tail, width), jnp.bfloat16)
    row = lax.broadcasted_iota(jnp.int32, (padded, LANES), 0)
    ones = jnp.where(row < tokens, 1.0, 0.0).astype(jnp.bfloat16)
    for pair in range(pairs):
        vals_scr[pair, tail:, :LANES] = jnp.zeros((padded - tail, LANES), jnp.bfloat16)
        vals_scr[pair, :, LANES:] = ones

    normed = layer_norm(partner.astype(jnp.float32), gains_ref[0:1, :]).astype(jnp.bfloat16)
    for start in range(0, width, MXU):
        keys_scr[:tokens, start : start + MXU] = head_unit(matmul(normed, qkv_ref[:, width + start : width + start + MXU]), block)
        value = matmul(normed, qkv_ref[:, 2 * width + start : 2 * width + start + MXU]).astype(jnp.bfloat16)
        for half in range(MXU // LANES):
            vals_scr[start // LANES + half, :tokens, :LANES] = value[:, half * LANES : (half + 1) * LANES]
    for pair in range(pairs):
        scores = lax.dot_general(
            q_ref[pair],
            keys_scr[:, pair * LANES : (pair + 1) * LANES],
            (((1,), (1,)), ((), ())),
            preferred_element_type=jnp.float32,
        )
        exponent = jnp.exp(scores * (TEMPER / head_size)).astype(jnp.bfloat16)
        mixed = matmul(exponent, vals_scr[pair])
        top = jnp.where(low_head, mixed[:tokens, :LANES], mixed[rows : rows + tokens, :LANES])
        norm = jnp.where(low_head, mixed[:tokens, LANES:], mixed[rows : rows + tokens, LANES:])
        att_scr[:, pair * LANES : (pair + 1) * LANES] = (top / norm).astype(jnp.bfloat16)
    for load in loads:
        load.wait()
    mixed = own_ref[...].astype(jnp.float32) + matmul(att_scr[...], out_ref[...])
    head_in = layer_norm(mixed, gains_ref[1:2, :]).astype(jnp.bfloat16)
    conf = matmul(head_in, head_ref[:, 3 * pixels :]) + bias_ref[:, 3 * pixels :]
    conf = conf.astype(jnp.bfloat16).astype(jnp.float32)
    weight = jnp.exp(CONF_RANGE * jnp.tanh(conf / CONF_RANGE)) * count_row
    for part in range(3):
        cols = slice(part * pixels, (part + 1) * pixels)
        xyz = matmul(head_in, head_ref[:, cols]) + bias_ref[:, cols]
        emit(part, cols, weight, weight * xyz.astype(jnp.bfloat16).astype(jnp.float32))


def view_scratch(tokens, width):
    padded, pairs = round_up(tokens, MXU), width // LANES
    return [
        pltpu.VMEM((padded, width), jnp.bfloat16),
        pltpu.VMEM((pairs, padded, MXU), jnp.bfloat16),
        pltpu.VMEM((tokens, width), jnp.bfloat16),
    ]


def first_kernel(
    scene_size,
    slots,
    offsets_of,
    tokens_hbm,
    qkv_hbm,
    attn_gain_hbm,
    head_gain_hbm,
    bias_hbm,
    list_hbm,
    count_hbm,
    own_ref,
    gains_ref,
    bias_ref,
    counts_ref,
    q_ref,
    wq_scr,
    list_smem,
    count_smem,
    sems,
):
    tokens, width = own_ref.shape
    head_size = width // HEADS
    rows = q_ref.shape[1] // 2
    plan = [
        (tokens_hbm.at[0], own_ref),
        (attn_gain_hbm, gains_ref.at[0]),
        (qkv_hbm.at[:, :width], wq_scr),
        (head_gain_hbm, gains_ref.at[1]),
        (bias_hbm, bias_ref.at[0]),
        (list_hbm, list_smem),
        (count_hbm, count_smem),
    ]
    copies = [pltpu.make_async_copy(source, target, sems.at[at]) for at, (source, target) in enumerate(plan)]
    for copy in copies:
        copy.start()
    for copy in copies[:3]:
        copy.wait()
    low_head = lax.broadcasted_iota(jnp.int32, (1, LANES), 1) < head_size
    block = head_block(head_size)
    normed = layer_norm(own_ref[...].astype(jnp.float32), gains_ref[0:1, :]).astype(jnp.bfloat16)
    q_ref[...] = jnp.zeros_like(q_ref)
    for start in range(0, width, MXU):
        unit = head_unit(matmul(normed, wq_scr[:, start : start + MXU]), block)
        for half in range(MXU // LANES):
            pair = start // LANES + half
            piece = unit[:, half * LANES : (half + 1) * LANES]
            zero = jnp.zeros_like(piece)
            q_ref[pair, :tokens, :] = jnp.where(low_head, piece, zero)
            q_ref[pair, rows : rows + tokens, :] = jnp.where(low_head, zero, piece)
    for copy in copies[3:]:
        copy.wait()
    position = lax.axis_index("scene")
    for at, offset in enumerate(offsets_of(position)):
        partner = lax.rem(position + offset + scene_size, scene_size)
        count = multiplicity(list_smem, count_smem, position, partner, slots).astype(jnp.float32)
        counts_ref[at] = jnp.full(counts_ref.shape[1:], count, jnp.float32)


def view_kernel(
    at, first, last, own_ref, gains_ref, bias_ref, counts_ref, q_ref, qkv_ref, out_ref, head_ref, partner_ref, *refs
):
    loads = ()
    if first:
        sums_ref, weights_ref, out_vmem, head_vmem, keys_scr, vals_scr, att_scr, load_sems = refs
        loads = (
            pltpu.make_async_copy(out_ref, out_vmem, load_sems.at[0]),
            pltpu.make_async_copy(head_ref, head_vmem, load_sems.at[1]),
        )
        for load in loads:
            load.start()
        out_ref, head_ref = out_vmem, head_vmem
    elif last:
        sums_in, weights_in, joined_hbm, keys_scr, vals_scr, att_scr, joined_scr, sems = refs
    else:
        sums_in, weights_in, sums_ref, weights_ref, keys_scr, vals_scr, att_scr = refs
    copies = []

    def emit(part, cols, weight, weighted):
        total = weighted if first else sums_in[:, cols] + weighted
        weight = weight if first else weights_in[...] + weight
        if last:
            joined_scr[:, cols] = total / weight
            copy = pltpu.make_async_copy(joined_scr.at[:, cols], joined_hbm.at[:, 0, cols], sems.at[part])
            copy.start()
            copies.append(copy)
        else:
            sums_ref[:, cols] = total
            if part == 0:
                weights_ref[...] = weight

    one_view(
        partner_ref[...], counts_ref[at, 0:1, 0:1], own_ref, q_ref, qkv_ref, out_ref, head_ref, gains_ref, bias_ref,
        keys_scr, vals_scr, att_scr, loads, emit,
    )
    for copy in copies:
        copy.wait()


def anchor_kernel(counts_in, weights_ref, counts_ref):
    counts_ref[...] = counts_in[...]


def per_device(
    tokens, qkv_weight, out_weight, attn_gain, head_gain, head_weight, head_bias, pair_list, pair_count
):
    scene_size = lax.axis_size("scene")
    _, token_count, width = tokens.shape
    slots = pair_list.shape[0] // scene_size
    columns = head_weight.shape[1]
    pixels = columns // 4
    f32, bf16 = jnp.float32, jnp.bfloat16
    own = tokens[0]

    def moved(value, target_of):
        return lax.ppermute(value, "scene", [(s, target_of(s) % scene_size) for s in range(scene_size)])

    def mate_of(s):
        return s ^ 1

    def offsets_of(position):
        to_mate = 1 - 2 * lax.rem(position, 2)
        return (to_mate, -to_mate, 2 * to_mate, -2 * to_mate)

    sums = jax.ShapeDtypeStruct((token_count, 3 * pixels), f32)
    weights = jax.ShapeDtypeStruct((token_count, pixels), f32)
    params = pltpu.CompilerParams(vmem_limit_bytes=24 * 2**20)
    cost = pl.CostEstimate(flops=4 * token_count * width * width * 2, bytes_accessed=2**20, transcendentals=0)

    alpha = moved(own, lambda s: s + 1 if s % 2 else s - 1)
    mate = moved(own, mate_of)
    first_shapes = (
        jax.ShapeDtypeStruct((token_count, width), bf16),
        jax.ShapeDtypeStruct((2, width), f32),
        jax.ShapeDtypeStruct((1, columns), f32),
        jax.ShapeDtypeStruct((4, 8, LANES), f32),
        jax.ShapeDtypeStruct((width // LANES, 2 * round_up(token_count, 16), LANES), bf16),
    )
    state = pl.pallas_call(
        functools.partial(first_kernel, scene_size, slots, offsets_of),
        out_shape=first_shapes,
        in_specs=[HBM_SPEC] * 7,
        out_specs=tuple(VMEM_SPEC for _ in first_shapes),
        scratch_shapes=[
            pltpu.VMEM((width, width), bf16),
            pltpu.SMEM((2, pair_list.shape[0]), jnp.int32),
            pltpu.SMEM(pair_count.shape, jnp.int32),
            pltpu.SemaphoreType.DMA((7,)),
        ],
        compiler_params=params,
        cost_estimate=pl.CostEstimate(flops=cost.flops, bytes_accessed=64 * 2**20, transcendentals=0),
        name="load_queries",
    )(
        in_hbm(tokens),
        *(in_hbm(value) for value in (qkv_weight, attn_gain, head_gain, head_bias)),
        in_hbm(pair_list.T),
        in_hbm(pair_count),
    )

    def view(at, partner, weights_now, totals, last=False):
        first = not totals
        operands = [*state, qkv_weight, *weights_now, partner, *totals]
        in_specs = [VMEM_SPEC] * len(operands)
        scratch = view_scratch(token_count, width)
        out_shape = [sums, weights]
        if first:
            out_shape += [jax.ShapeDtypeStruct(value.shape, value.dtype) for value in weights_now]
            in_specs[6:8] = [HBM_SPEC] * 2
            scratch += [pltpu.SemaphoreType.DMA((2,))]
        if last:
            out_shape = [jax.ShapeDtypeStruct((token_count, 1, 3 * pixels), f32)]
            scratch += [pltpu.VMEM(sums.shape, f32), pltpu.SemaphoreType.DMA((3,))]
        return pl.pallas_call(
            functools.partial(view_kernel, at, first, last),
            out_shape=out_shape,
            in_specs=in_specs,
            out_specs=[HBM_SPEC if last else VMEM_SPEC] * len(out_shape),
            scratch_shapes=scratch,
            compiler_params=params,
            cost_estimate=cost,
        )(*operands)

    *totals, out_vmem, head_vmem = view(0, mate, (in_hbm(out_weight), in_hbm(head_weight)), ())
    weights_now = (out_vmem, head_vmem)
    own, *totals = lax.optimization_barrier((own, *totals))
    beta = moved(own, lambda s: s - 2 if s % 2 else s + 2)
    counts = pl.pallas_call(
        anchor_kernel,
        out_shape=first_shapes[3],
        in_specs=[VMEM_SPEC] * 2,
        out_specs=VMEM_SPEC,
        compiler_params=params,
        name="anchor",
    )(state[3], totals[1])
    state = (*state[:3], counts, state[4])
    alpha, *totals = lax.optimization_barrier((alpha, *totals))
    swapped = moved(alpha, mate_of)
    totals = view(1, alpha, weights_now, totals)
    totals = view(2, swapped, weights_now, totals)
    return view(3, beta, weights_now, totals, last=True)[0].transpose(1, 0, 2)


def solution(mesh):
    return jax.shard_map(
        per_device,
        mesh=mesh,
        in_specs=(
            P(("groups", "scene"), None, None),
            P(),
            P(),
            P(),
            P(),
            P(),
            P(),
            P("groups", None),
            P("groups"),
        ),
        out_specs=P(("groups", "scene"), None, None),
        check_vma=False,
    )
```

```python
import functools

import jax
import jax.numpy as jnp
from jax import lax
from jax.experimental import pallas as pl
from jax.experimental.pallas import tpu as pltpu
from jax.sharding import PartitionSpec as P


HEADS = 12
TEMPER = 16.0
CONF_RANGE = 4.0
EPSILON = 1e-06
LANES = 128
MXU = 256

VMEM_SPEC = pl.BlockSpec(memory_space=pltpu.VMEM)
HBM_SPEC = pl.BlockSpec(memory_space=pltpu.HBM)


def in_hbm(value):
    return pltpu.with_memory_space_constraint(value, pltpu.HBM)


def round_up(value, step):
    return -(-value // step) * step


def layer_norm(values, gain_row):
    centred = values - jnp.mean(values, axis=-1, keepdims=True)
    spread = jnp.mean(centred * centred, axis=-1, keepdims=True)
    return centred * lax.rsqrt(spread + EPSILON) * gain_row


def matmul(left, right):
    return jnp.dot(left, right, preferred_element_type=jnp.float32)


def head_block(head_size):
    rows = lax.broadcasted_iota(jnp.int32, (MXU, MXU), 0) // head_size
    cols = lax.broadcasted_iota(jnp.int32, (MXU, MXU), 1) // head_size
    return jnp.where(rows == cols, 1.0 / head_size, 0.0).astype(jnp.bfloat16)


def head_unit(mixed, block):
    energy = matmul((mixed * mixed).astype(jnp.bfloat16), block)
    return (mixed * lax.rsqrt(energy + EPSILON)).astype(jnp.bfloat16)


def multiplicity(pair_list, pair_count, own, partner, slots):
    count = jnp.int32(0)
    for slot in range(slots):
        for first, second in ((own, partner), (partner, own)):
            live = slot < pair_count[first]
            hit = pair_list[1, first * slots + slot] == second
            count = count + jnp.where(jnp.logical_and(live, hit), 1, 0)
    return count


def one_view(normed, count_row, own_ref, q_ref, kv_ref, out_ref, head_ref, gains_ref, bias_ref, keys_scr, vals_scr, att_scr, loads, emit):
    tokens, width = own_ref.shape
    head_size = width // HEADS
    pixels = head_ref.shape[1] // 4
    rows = q_ref.shape[1] // 2
    padded = keys_scr.shape[0]
    pairs = width // LANES
    low_head = lax.broadcasted_iota(jnp.int32, (1, LANES), 1) < head_size
    block = head_block(head_size)

    tail = tokens // 16 * 16
    keys_scr[tail:, :] = jnp.zeros((padded - tail, width), jnp.bfloat16)
    row = lax.broadcasted_iota(jnp.int32, (padded, LANES), 0)
    ones = jnp.where(row < tokens, 1.0, 0.0).astype(jnp.bfloat16)
    for pair in range(pairs):
        vals_scr[pair, tail:, :LANES] = jnp.zeros((padded - tail, LANES), jnp.bfloat16)
        vals_scr[pair, :, LANES:] = ones

    for start in range(0, width, MXU):
        keys_scr[:tokens, start : start + MXU] = head_unit(matmul(normed, kv_ref[:, start : start + MXU]), block)
        value = matmul(normed, kv_ref[:, width + start : width + start + MXU]).astype(jnp.bfloat16)
        for half in range(MXU // LANES):
            vals_scr[start // LANES + half, :tokens, :LANES] = value[:, half * LANES : (half + 1) * LANES]
    for pair in range(pairs):
        scores = lax.dot_general(
            q_ref[pair],
            keys_scr[:, pair * LANES : (pair + 1) * LANES],
            (((1,), (1,)), ((), ())),
            preferred_element_type=jnp.float32,
        )
        exponent = jnp.exp(scores * (TEMPER / head_size)).astype(jnp.bfloat16)
        mixed = matmul(exponent, vals_scr[pair])
        top = jnp.where(low_head, mixed[:tokens, :LANES], mixed[rows : rows + tokens, :LANES])
        norm = jnp.where(low_head, mixed[:tokens, LANES:], mixed[rows : rows + tokens, LANES:])
        att_scr[:, pair * LANES : (pair + 1) * LANES] = (top / norm).astype(jnp.bfloat16)
    for load in loads:
        load.wait()
    mixed = own_ref[...].astype(jnp.float32) + matmul(att_scr[...], out_ref[...])
    head_in = layer_norm(mixed, gains_ref[1:2, :]).astype(jnp.bfloat16)
    conf = matmul(head_in, head_ref[:, 3 * pixels :]) + bias_ref[:, 3 * pixels :]
    conf = conf.astype(jnp.bfloat16).astype(jnp.float32)
    weight = jnp.exp(CONF_RANGE * jnp.tanh(conf / CONF_RANGE)) * count_row
    for part in range(3):
        cols = slice(part * pixels, (part + 1) * pixels)
        xyz = matmul(head_in, head_ref[:, cols]) + bias_ref[:, cols]
        emit(part, cols, weight, weight * xyz.astype(jnp.bfloat16).astype(jnp.float32))


def view_scratch(tokens, width):
    padded, pairs = round_up(tokens, MXU), width // LANES
    return [
        pltpu.VMEM((padded, width), jnp.bfloat16),
        pltpu.VMEM((pairs, padded, MXU), jnp.bfloat16),
        pltpu.VMEM((tokens, width), jnp.bfloat16),
    ]


def first_kernel(
    scene_size,
    slots,
    offsets_of,
    tokens_hbm,
    qkv_hbm,
    attn_gain_hbm,
    head_gain_hbm,
    bias_hbm,
    list_hbm,
    count_hbm,
    own_ref,
    normed_ref,
    kv_ref,
    gains_ref,
    bias_ref,
    counts_ref,
    q_ref,
    wq_scr,
    list_smem,
    count_smem,
    sems,
):
    tokens, width = own_ref.shape
    head_size = width // HEADS
    rows = q_ref.shape[1] // 2
    first_cols = [slice(start, start + MXU) for start in range(0, width, MXU)]
    plan = [
        (tokens_hbm.at[0], own_ref),
        (attn_gain_hbm, gains_ref.at[0]),
        *((qkv_hbm.at[:, cols], wq_scr.at[:, cols]) for cols in first_cols),
        (list_hbm, list_smem),
        (count_hbm, count_smem),
        (head_gain_hbm, gains_ref.at[1]),
        (bias_hbm, bias_ref.at[0]),
        (qkv_hbm.at[:, width : 2 * width], kv_ref.at[:, :width]),
        (qkv_hbm.at[:, 2 * width :], kv_ref.at[:, width:]),
    ]
    copies = [pltpu.make_async_copy(source, target, sems.at[at]) for at, (source, target) in enumerate(plan)]
    for copy in copies:
        copy.start()
    low_head = lax.broadcasted_iota(jnp.int32, (1, LANES), 1) < head_size
    block = head_block(head_size)
    tail = tokens // 16 * 16
    for half in range(2):
        q_ref[:, half * rows + tail : (half + 1) * rows, :] = jnp.zeros((q_ref.shape[0], rows - tail, LANES), jnp.bfloat16)
    for copy in copies[:2]:
        copy.wait()
    normed_ref[...] = layer_norm(own_ref[...].astype(jnp.float32), gains_ref[0:1, :]).astype(jnp.bfloat16)
    normed = normed_ref[...]
    for at, cols in enumerate(first_cols):
        copies[2 + at].wait()
        unit = head_unit(matmul(normed, wq_scr[:, cols]), block)
        for half in range(MXU // LANES):
            pair = cols.start // LANES + half
            piece = unit[:, half * LANES : (half + 1) * LANES]
            zero = jnp.zeros_like(piece)
            q_ref[pair, :tokens, :] = jnp.where(low_head, piece, zero)
            q_ref[pair, rows : rows + tokens, :] = jnp.where(low_head, zero, piece)
    for copy in copies[2 + len(first_cols) :]:
        copy.wait()
    position = lax.axis_index("scene")
    for at, offset in enumerate(offsets_of(position)):
        partner = lax.rem(position + offset + scene_size, scene_size)
        count = multiplicity(list_smem, count_smem, position, partner, slots).astype(jnp.float32)
        counts_ref[at] = jnp.full(counts_ref.shape[1:], count, jnp.float32)


def view_kernel(
    at, first, last, own_ref, gains_ref, bias_ref, counts_ref, q_ref, kv_ref, out_ref, head_ref, partner_ref, *refs
):
    loads = ()
    if first:
        sums_ref, weights_ref, out_vmem, head_vmem, keys_scr, vals_scr, att_scr, load_sems = refs
        loads = (
            pltpu.make_async_copy(out_ref, out_vmem, load_sems.at[0]),
            pltpu.make_async_copy(head_ref, head_vmem, load_sems.at[1]),
        )
        for load in loads:
            load.start()
        out_ref, head_ref = out_vmem, head_vmem
    elif last:
        sums_in, weights_in, joined_hbm, keys_scr, vals_scr, att_scr, joined_scr, sems = refs
    else:
        sums_in, weights_in, sums_ref, weights_ref, keys_scr, vals_scr, att_scr = refs
    copies = []

    def emit(part, cols, weight, weighted):
        total = weighted if first else sums_in[:, cols] + weighted
        weight = weight if first else weights_in[...] + weight
        if last:
            ratio = total / weight
            lines = 3 * total.shape[1] // LANES
            for line in range(total.shape[1] // LANES):
                rows = pl.ds(cols.start // LANES + line, total.shape[0], stride=lines)
                joined_scr[rows, :] = ratio[:, line * LANES : (line + 1) * LANES]
            if part == 2:
                copy = pltpu.make_async_copy(joined_scr, joined_hbm, sems.at[0])
                copy.start()
                copies.append(copy)
        else:
            sums_ref[:, cols] = total
            if part == 0:
                weights_ref[...] = weight

    normed = partner_ref[...]
    if not last:
        normed = layer_norm(normed.astype(jnp.float32), gains_ref[0:1, :]).astype(jnp.bfloat16)
    one_view(
        normed, counts_ref[at, 0:1, 0:1], own_ref, q_ref, kv_ref, out_ref, head_ref, gains_ref, bias_ref,
        keys_scr, vals_scr, att_scr, loads, emit,
    )
    for copy in copies:
        copy.wait()


def anchor_kernel(counts_in, weights_ref, counts_ref):
    counts_ref[...] = counts_in[...]


def per_device(
    tokens, qkv_weight, out_weight, attn_gain, head_gain, head_weight, head_bias, pair_list, pair_count
):
    scene_size = lax.axis_size("scene")
    _, token_count, width = tokens.shape
    slots = pair_list.shape[0] // scene_size
    columns = head_weight.shape[1]
    pixels = columns // 4
    f32, bf16 = jnp.float32, jnp.bfloat16
    own = tokens[0]

    def moved(value, target_of):
        return lax.ppermute(value, "scene", [(s, target_of(s) % scene_size) for s in range(scene_size)])

    def mate_of(s):
        return s ^ 1

    def offsets_of(position):
        to_mate = 1 - 2 * lax.rem(position, 2)
        return (to_mate, -to_mate, 2 * to_mate, -2 * to_mate)

    sums = jax.ShapeDtypeStruct((token_count, 3 * pixels), f32)
    weights = jax.ShapeDtypeStruct((token_count, pixels), f32)
    params = pltpu.CompilerParams(vmem_limit_bytes=24 * 2**20)
    cost = pl.CostEstimate(flops=4 * token_count * width * width * 2, bytes_accessed=2**20, transcendentals=0)

    alpha = moved(own, lambda s: s + 1 if s % 2 else s - 1)
    mate = moved(own, mate_of)
    first_shapes = (
        jax.ShapeDtypeStruct((token_count, width), bf16),
        jax.ShapeDtypeStruct((token_count, width), bf16),
        jax.ShapeDtypeStruct((width, 2 * width), bf16),
        jax.ShapeDtypeStruct((2, width), f32),
        jax.ShapeDtypeStruct((1, columns), f32),
        jax.ShapeDtypeStruct((4, 8, LANES), f32),
        jax.ShapeDtypeStruct((width // LANES, 2 * round_up(token_count, 16), LANES), bf16),
    )
    own_vmem, normed, kv_vmem, gains, bias, counts, queries = pl.pallas_call(
        functools.partial(first_kernel, scene_size, slots, offsets_of),
        out_shape=first_shapes,
        in_specs=[HBM_SPEC] * 7,
        out_specs=tuple(VMEM_SPEC for _ in first_shapes),
        scratch_shapes=[
            pltpu.VMEM((width, width), bf16),
            pltpu.SMEM((2, pair_list.shape[0]), jnp.int32),
            pltpu.SMEM(pair_count.shape, jnp.int32),
            pltpu.SemaphoreType.DMA((8 + width // MXU,)),
        ],
        compiler_params=params,
        cost_estimate=cost,
        name="load_queries",
    )(
        in_hbm(tokens),
        *(in_hbm(value) for value in (qkv_weight, attn_gain, head_gain, head_bias)),
        in_hbm(pair_list.T),
        in_hbm(pair_count),
    )

    def view(at, partner, counts_now, weights_now, totals, last=False):
        first = not totals
        operands = [own_vmem, gains, bias, counts_now, queries, kv_vmem, *weights_now, partner, *totals]
        in_specs = [VMEM_SPEC] * len(operands)
        scratch = view_scratch(token_count, width)
        out_shape = [sums, weights]
        if first:
            out_shape += [jax.ShapeDtypeStruct(value.shape, value.dtype) for value in weights_now]
            in_specs[6:8] = [HBM_SPEC] * 2
            scratch += [pltpu.SemaphoreType.DMA((2,))]
        if last:
            out_shape = [jax.ShapeDtypeStruct((token_count * 3 * pixels // LANES, LANES), f32)]
            scratch += [pltpu.VMEM(out_shape[0].shape, f32), pltpu.SemaphoreType.DMA((1,))]
        return pl.pallas_call(
            functools.partial(view_kernel, at, first, last),
            out_shape=out_shape,
            in_specs=in_specs,
            out_specs=[HBM_SPEC if last else VMEM_SPEC] * len(out_shape),
            scratch_shapes=scratch,
            compiler_params=params,
            cost_estimate=cost,
        )(*operands)

    *totals, out_vmem, head_vmem = view(0, mate, counts, (in_hbm(out_weight), in_hbm(head_weight)), ())
    weights_now = (out_vmem, head_vmem)
    normed, *totals = lax.optimization_barrier((normed, *totals))
    beta = moved(normed, lambda s: s - 2 if s % 2 else s + 2)
    counts_now = pl.pallas_call(
        anchor_kernel,
        out_shape=first_shapes[5],
        in_specs=[VMEM_SPEC] * 2,
        out_specs=VMEM_SPEC,
        compiler_params=params,
        name="anchor",
    )(counts, totals[1])
    alpha, *totals = lax.optimization_barrier((alpha, *totals))
    swapped = moved(alpha, mate_of)
    totals = view(1, alpha, counts_now, weights_now, totals)
    totals = view(2, swapped, counts_now, weights_now, totals)
    return view(3, beta, counts_now, weights_now, totals, last=True)[0].reshape(1, token_count, 3 * pixels)


def solution(mesh):
    return jax.shard_map(
        per_device,
        mesh=mesh,
        in_specs=(
            P(("groups", "scene"), None, None),
            P(),
            P(),
            P(),
            P(),
            P(),
            P(),
            P("groups", None),
            P("groups"),
        ),
        out_specs=P(("groups", "scene"), None, None),
        check_vma=False,
    )
```

```python
import functools

import jax
import jax.numpy as jnp
from jax import lax
from jax.experimental import pallas as pl
from jax.experimental.pallas import tpu as pltpu
from jax.sharding import PartitionSpec as P


HEADS = 12
TEMPER = 16.0
CONF_RANGE = 4.0
EPSILON = 1e-06
LANES = 128
MXU = 256

VMEM_SPEC = pl.BlockSpec(memory_space=pltpu.VMEM)
HBM_SPEC = pl.BlockSpec(memory_space=pltpu.HBM)


def in_hbm(value):
    return pltpu.with_memory_space_constraint(value, pltpu.HBM)


def round_up(value, step):
    return -(-value // step) * step


def layer_norm(values, gain_row):
    centred = values - jnp.mean(values, axis=-1, keepdims=True)
    spread = jnp.mean(centred * centred, axis=-1, keepdims=True)
    return centred * lax.rsqrt(spread + EPSILON) * gain_row


def matmul(left, right):
    return jnp.dot(left, right, preferred_element_type=jnp.float32)


def head_block(head_size):
    rows = lax.broadcasted_iota(jnp.int32, (MXU, MXU), 0) // head_size
    cols = lax.broadcasted_iota(jnp.int32, (MXU, MXU), 1) // head_size
    return jnp.where(rows == cols, 1.0 / head_size, 0.0).astype(jnp.bfloat16)


def head_unit(mixed, block):
    energy = matmul((mixed * mixed).astype(jnp.bfloat16), block)
    return (mixed * lax.rsqrt(energy + EPSILON)).astype(jnp.bfloat16)


def multiplicity(pair_list, pair_count, own, partner, slots):
    count = jnp.int32(0)
    for slot in range(slots):
        for first, second in ((own, partner), (partner, own)):
            live = slot < pair_count[first]
            hit = pair_list[1, first * slots + slot] == second
            count = count + jnp.where(jnp.logical_and(live, hit), 1, 0)
    return count


def attend(normed, q_ref, kv_ref, keys_scr, vals_scr, att_ref):
    tokens, width = normed.shape
    head_size = width // HEADS
    rows = q_ref.shape[1] // 2
    padded = keys_scr.shape[0]
    pairs = width // LANES
    low_head = lax.broadcasted_iota(jnp.int32, (1, LANES), 1) < head_size
    block = head_block(head_size)

    tail = tokens // 16 * 16
    keys_scr[tail:, :] = jnp.zeros((padded - tail, width), jnp.bfloat16)
    row = lax.broadcasted_iota(jnp.int32, (padded, LANES), 0)
    ones = jnp.where(row < tokens, 1.0, 0.0).astype(jnp.bfloat16)
    for pair in range(pairs):
        vals_scr[pair, tail:, :LANES] = jnp.zeros((padded - tail, LANES), jnp.bfloat16)
        vals_scr[pair, :, LANES:] = ones

    for start in range(0, width, MXU):
        keys_scr[:tokens, start : start + MXU] = head_unit(matmul(normed, kv_ref[:, start : start + MXU]), block)
        value = matmul(normed, kv_ref[:, width + start : width + start + MXU]).astype(jnp.bfloat16)
        for half in range(MXU // LANES):
            vals_scr[start // LANES + half, :tokens, :LANES] = value[:, half * LANES : (half + 1) * LANES]
    for pair in range(pairs):
        scores = lax.dot_general(
            q_ref[pair],
            keys_scr[:, pair * LANES : (pair + 1) * LANES],
            (((1,), (1,)), ((), ())),
            preferred_element_type=jnp.float32,
        )
        exponent = jnp.exp(scores * (TEMPER / head_size)).astype(jnp.bfloat16)
        mixed = matmul(exponent, vals_scr[pair])
        top = jnp.where(low_head, mixed[:tokens, :LANES], mixed[rows : rows + tokens, :LANES])
        norm = jnp.where(low_head, mixed[:tokens, LANES:], mixed[rows : rows + tokens, LANES:])
        att_ref[:, pair * LANES : (pair + 1) * LANES] = (top / norm).astype(jnp.bfloat16)


def finish(attended, count_row, own_ref, out_ref, head_ref, gains_ref, bias_ref, emit):
    pixels = head_ref.shape[1] // 4
    mixed = own_ref[...].astype(jnp.float32) + matmul(attended, out_ref[...])
    head_in = layer_norm(mixed, gains_ref[1:2, :]).astype(jnp.bfloat16)
    conf = matmul(head_in, head_ref[:, 3 * pixels :]) + bias_ref[:, 3 * pixels :]
    conf = conf.astype(jnp.bfloat16).astype(jnp.float32)
    weight = jnp.exp(CONF_RANGE * jnp.tanh(conf / CONF_RANGE)) * count_row
    for part in range(3):
        cols = slice(part * pixels, (part + 1) * pixels)
        xyz = matmul(head_in, head_ref[:, cols]) + bias_ref[:, cols]
        emit(part, cols, weight, weight * xyz.astype(jnp.bfloat16).astype(jnp.float32))


def view_scratch(tokens, width):
    padded, pairs = round_up(tokens, MXU), width // LANES
    return [
        pltpu.VMEM((padded, width), jnp.bfloat16),
        pltpu.VMEM((pairs, padded, MXU), jnp.bfloat16),
        pltpu.VMEM((tokens, width), jnp.bfloat16),
    ]


def first_kernel(
    scene_size,
    slots,
    offsets_of,
    tokens_hbm,
    qkv_hbm,
    attn_gain_hbm,
    head_gain_hbm,
    bias_hbm,
    list_hbm,
    count_hbm,
    own_ref,
    normed_ref,
    kv_ref,
    gains_ref,
    bias_ref,
    counts_ref,
    q_ref,
    wq_scr,
    list_smem,
    count_smem,
    sems,
):
    tokens, width = own_ref.shape
    head_size = width // HEADS
    rows = q_ref.shape[1] // 2
    first_cols = [slice(start, start + MXU) for start in range(0, width, MXU)]
    plan = [
        (tokens_hbm.at[0], own_ref),
        (attn_gain_hbm, gains_ref.at[0]),
        *((qkv_hbm.at[:, cols], wq_scr.at[:, cols]) for cols in first_cols),
        (list_hbm, list_smem),
        (count_hbm, count_smem),
        (head_gain_hbm, gains_ref.at[1]),
        (bias_hbm, bias_ref.at[0]),
        (qkv_hbm.at[:, width : 2 * width], kv_ref.at[:, :width]),
        (qkv_hbm.at[:, 2 * width :], kv_ref.at[:, width:]),
    ]
    copies = [pltpu.make_async_copy(source, target, sems.at[at]) for at, (source, target) in enumerate(plan)]
    for copy in copies:
        copy.start()
    low_head = lax.broadcasted_iota(jnp.int32, (1, LANES), 1) < head_size
    block = head_block(head_size)
    tail = tokens // 16 * 16
    for half in range(2):
        q_ref[:, half * rows + tail : (half + 1) * rows, :] = jnp.zeros((q_ref.shape[0], rows - tail, LANES), jnp.bfloat16)
    for copy in copies[:2]:
        copy.wait()
    normed_ref[...] = layer_norm(own_ref[...].astype(jnp.float32), gains_ref[0:1, :]).astype(jnp.bfloat16)
    normed = normed_ref[...]
    for at, cols in enumerate(first_cols):
        copies[2 + at].wait()
        unit = head_unit(matmul(normed, wq_scr[:, cols]), block)
        for half in range(MXU // LANES):
            pair = cols.start // LANES + half
            piece = unit[:, half * LANES : (half + 1) * LANES]
            zero = jnp.zeros_like(piece)
            q_ref[pair, :tokens, :] = jnp.where(low_head, piece, zero)
            q_ref[pair, rows : rows + tokens, :] = jnp.where(low_head, zero, piece)
    for copy in copies[2 + len(first_cols) :]:
        copy.wait()
    position = lax.axis_index("scene")
    for at, offset in enumerate(offsets_of(position)):
        partner = lax.rem(position + offset + scene_size, scene_size)
        count = multiplicity(list_smem, count_smem, position, partner, slots).astype(jnp.float32)
        counts_ref[at] = jnp.full(counts_ref.shape[1:], count, jnp.float32)


def mate_kernel(gains_ref, q_ref, kv_ref, partner_ref, att_ref, keys_scr, vals_scr):
    normed = layer_norm(partner_ref[...].astype(jnp.float32), gains_ref[0:1, :]).astype(jnp.bfloat16)
    attend(normed, q_ref, kv_ref, keys_scr, vals_scr, att_ref)


def mate_maps_kernel(own_ref, gains_ref, bias_ref, counts_ref, att_ref, out_ref, head_ref, sums_ref, weights_ref):
    def emit(part, cols, weight, weighted):
        sums_ref[:, cols] = weighted
        if part == 0:
            weights_ref[...] = weight

    finish(att_ref[...], counts_ref[0, 0:1, 0:1], own_ref, out_ref, head_ref, gains_ref, bias_ref, emit)


def view_kernel(at, last, own_ref, gains_ref, bias_ref, counts_ref, q_ref, kv_ref, out_ref, head_ref, partner_ref, *refs):
    if last:
        sums_in, weights_in, joined_hbm, keys_scr, vals_scr, att_scr, joined_scr, sems = refs
    else:
        sums_in, weights_in, sums_ref, weights_ref, keys_scr, vals_scr, att_scr = refs
    copies = []

    def emit(part, cols, weight, weighted):
        total = sums_in[:, cols] + weighted
        weight = weights_in[...] + weight
        if last:
            ratio = total / weight
            lines = 3 * total.shape[1] // LANES
            for line in range(total.shape[1] // LANES):
                rows = pl.ds(cols.start // LANES + line, total.shape[0], stride=lines)
                joined_scr[rows, :] = ratio[:, line * LANES : (line + 1) * LANES]
            if part == 2:
                copy = pltpu.make_async_copy(joined_scr, joined_hbm, sems.at[0])
                copy.start()
                copies.append(copy)
        else:
            sums_ref[:, cols] = total
            if part == 0:
                weights_ref[...] = weight

    normed = partner_ref[...]
    if not last:
        normed = layer_norm(normed.astype(jnp.float32), gains_ref[0:1, :]).astype(jnp.bfloat16)
    attend(normed, q_ref, kv_ref, keys_scr, vals_scr, att_scr)
    finish(att_scr[...], counts_ref[at, 0:1, 0:1], own_ref, out_ref, head_ref, gains_ref, bias_ref, emit)
    for copy in copies:
        copy.wait()


def per_device(
    tokens, qkv_weight, out_weight, attn_gain, head_gain, head_weight, head_bias, pair_list, pair_count
):
    scene_size = lax.axis_size("scene")
    _, token_count, width = tokens.shape
    slots = pair_list.shape[0] // scene_size
    columns = head_weight.shape[1]
    pixels = columns // 4
    f32, bf16 = jnp.float32, jnp.bfloat16
    own = tokens[0]

    def moved(value, target_of):
        return lax.ppermute(value, "scene", [(s, target_of(s) % scene_size) for s in range(scene_size)])

    def mate_of(s):
        return s ^ 1

    def offsets_of(position):
        to_mate = 1 - 2 * lax.rem(position, 2)
        return (to_mate, -to_mate, 2 * to_mate, -2 * to_mate)

    sums = jax.ShapeDtypeStruct((token_count, 3 * pixels), f32)
    weights = jax.ShapeDtypeStruct((token_count, pixels), f32)
    params = pltpu.CompilerParams(vmem_limit_bytes=24 * 2**20)
    cost = pl.CostEstimate(flops=4 * token_count * width * width * 2, bytes_accessed=2**20, transcendentals=0)

    alpha = moved(own, lambda s: s + 1 if s % 2 else s - 1)
    mate = moved(own, mate_of)
    first_shapes = (
        jax.ShapeDtypeStruct((token_count, width), bf16),
        jax.ShapeDtypeStruct((token_count, width), bf16),
        jax.ShapeDtypeStruct((width, 2 * width), bf16),
        jax.ShapeDtypeStruct((2, width), f32),
        jax.ShapeDtypeStruct((1, columns), f32),
        jax.ShapeDtypeStruct((4, 8, LANES), f32),
        jax.ShapeDtypeStruct((width // LANES, 2 * round_up(token_count, 16), LANES), bf16),
    )
    own_vmem, normed, kv_vmem, gains, bias, counts, queries = pl.pallas_call(
        functools.partial(first_kernel, scene_size, slots, offsets_of),
        out_shape=first_shapes,
        in_specs=[HBM_SPEC] * 7,
        out_specs=tuple(VMEM_SPEC for _ in first_shapes),
        scratch_shapes=[
            pltpu.VMEM((width, width), bf16),
            pltpu.SMEM((2, pair_list.shape[0]), jnp.int32),
            pltpu.SMEM(pair_count.shape, jnp.int32),
            pltpu.SemaphoreType.DMA((8 + width // MXU,)),
        ],
        compiler_params=params,
        cost_estimate=cost,
        name="load_queries",
    )(
        in_hbm(tokens),
        *(in_hbm(value) for value in (qkv_weight, attn_gain, head_gain, head_bias)),
        in_hbm(pair_list.T),
        in_hbm(pair_count),
    )

    def kernel(body, operands, in_specs, out_shape, out_spec, scratch):
        return pl.pallas_call(
            body,
            out_shape=out_shape,
            in_specs=in_specs,
            out_specs=[out_spec] * len(out_shape),
            scratch_shapes=scratch,
            compiler_params=params,
            cost_estimate=cost,
        )(*operands)

    scratch = view_scratch(token_count, width)
    (attended,) = kernel(
        mate_kernel,
        (gains, queries, kv_vmem, mate),
        [VMEM_SPEC] * 4,
        [jax.ShapeDtypeStruct((token_count, width), bf16)],
        VMEM_SPEC,
        scratch[:2],
    )
    normed, attended = lax.optimization_barrier((normed, attended))
    beta = moved(normed, lambda s: s - 2 if s % 2 else s + 2)
    totals = kernel(
        mate_maps_kernel,
        (own_vmem, gains, bias, counts, attended, out_weight, head_weight),
        [VMEM_SPEC] * 7,
        (sums, weights),
        VMEM_SPEC,
        [],
    )
    alpha, *totals = lax.optimization_barrier((alpha, *totals))
    swapped = moved(alpha, mate_of)
    common = (own_vmem, gains, bias, counts, queries, kv_vmem, out_weight, head_weight)
    for at, partner in ((1, alpha), (2, swapped)):
        totals = kernel(
            functools.partial(view_kernel, at, False),
            (*common, partner, *totals),
            [VMEM_SPEC] * 11,
            (sums, weights),
            VMEM_SPEC,
            scratch,
        )
    joined_shape = jax.ShapeDtypeStruct((token_count * 3 * pixels // LANES, LANES), f32)
    (joined,) = kernel(
        functools.partial(view_kernel, 3, True),
        (*common, beta, *totals),
        [VMEM_SPEC] * 11,
        (joined_shape,),
        HBM_SPEC,
        scratch + [pltpu.VMEM(joined_shape.shape, f32), pltpu.SemaphoreType.DMA((1,))],
    )
    return joined.reshape(1, token_count, 3 * pixels)


def solution(mesh):
    return jax.shard_map(
        per_device,
        mesh=mesh,
        in_specs=(
            P(("groups", "scene"), None, None),
            P(),
            P(),
            P(),
            P(),
            P(),
            P(),
            P("groups", None),
            P("groups"),
        ),
        out_specs=P(("groups", "scene"), None, None),
        check_vma=False,
    )
```

```python
import functools

import jax
import jax.numpy as jnp
from jax import lax
from jax.experimental import pallas as pl
from jax.experimental.pallas import tpu as pltpu
from jax.sharding import PartitionSpec as P


HEADS = 12
TEMPER = 16.0
CONF_RANGE = 4.0
EPSILON = 1e-06
LANES = 128
MXU = 256

VMEM_SPEC = pl.BlockSpec(memory_space=pltpu.VMEM)
HBM_SPEC = pl.BlockSpec(memory_space=pltpu.HBM)


def in_hbm(value):
    return pltpu.with_memory_space_constraint(value, pltpu.HBM)


def round_up(value, step):
    return -(-value // step) * step


def layer_norm(values, gain_row):
    centred = values - jnp.mean(values, axis=-1, keepdims=True)
    spread = jnp.mean(centred * centred, axis=-1, keepdims=True)
    return centred * lax.rsqrt(spread + EPSILON) * gain_row


def matmul(left, right):
    return jnp.dot(left, right, preferred_element_type=jnp.float32)


def head_block(head_size):
    rows = lax.broadcasted_iota(jnp.int32, (MXU, MXU), 0) // head_size
    cols = lax.broadcasted_iota(jnp.int32, (MXU, MXU), 1) // head_size
    return jnp.where(rows == cols, 1.0 / head_size, 0.0).astype(jnp.bfloat16)


def head_unit(mixed, block):
    energy = matmul((mixed * mixed).astype(jnp.bfloat16), block)
    return (mixed * lax.rsqrt(energy + EPSILON)).astype(jnp.bfloat16)


def multiplicity(pair_list, pair_count, own, partner, slots):
    count = jnp.int32(0)
    for slot in range(slots):
        for first, second in ((own, partner), (partner, own)):
            live = slot < pair_count[first]
            hit = pair_list[1, first * slots + slot] == second
            count = count + jnp.where(jnp.logical_and(live, hit), 1, 0)
    return count


def attend(normed, q_ref, kv_ref, keys_scr, vals_scr, att_ref):
    tokens, width = normed.shape
    head_size = width // HEADS
    rows = q_ref.shape[1] // 2
    padded = keys_scr.shape[0]
    pairs = width // LANES
    low_head = lax.broadcasted_iota(jnp.int32, (1, LANES), 1) < head_size
    block = head_block(head_size)

    tail = tokens // 16 * 16
    keys_scr[tail:, :] = jnp.zeros((padded - tail, width), jnp.bfloat16)
    row = lax.broadcasted_iota(jnp.int32, (padded, LANES), 0)
    ones = jnp.where(row < tokens, 1.0, 0.0).astype(jnp.bfloat16)
    for pair in range(pairs):
        vals_scr[pair, tail:, :LANES] = jnp.zeros((padded - tail, LANES), jnp.bfloat16)
        vals_scr[pair, :, LANES:] = ones

    for start in range(0, width, MXU):
        keys_scr[:tokens, start : start + MXU] = head_unit(matmul(normed, kv_ref[:, start : start + MXU]), block)
        value = matmul(normed, kv_ref[:, width + start : width + start + MXU]).astype(jnp.bfloat16)
        for half in range(MXU // LANES):
            vals_scr[start // LANES + half, :tokens, :LANES] = value[:, half * LANES : (half + 1) * LANES]
    for pair in range(pairs):
        scores = lax.dot_general(
            q_ref[pair],
            keys_scr[:, pair * LANES : (pair + 1) * LANES],
            (((1,), (1,)), ((), ())),
            preferred_element_type=jnp.float32,
        )
        exponent = jnp.exp(scores * (TEMPER / head_size)).astype(jnp.bfloat16)
        mixed = matmul(exponent, vals_scr[pair])
        top = jnp.where(low_head, mixed[:tokens, :LANES], mixed[rows : rows + tokens, :LANES])
        norm = jnp.where(low_head, mixed[:tokens, LANES:], mixed[rows : rows + tokens, LANES:])
        att_ref[:, pair * LANES : (pair + 1) * LANES] = (top / norm).astype(jnp.bfloat16)


def finish(attended, count_row, own_ref, out_ref, head_ref, gains_ref, bias_ref, emit):
    pixels = head_ref.shape[1] // 4
    mixed = own_ref[...].astype(jnp.float32) + matmul(attended, out_ref[...])
    head_in = layer_norm(mixed, gains_ref[1:2, :]).astype(jnp.bfloat16)
    conf = matmul(head_in, head_ref[:, 3 * pixels :]) + bias_ref[:, 3 * pixels :]
    conf = conf.astype(jnp.bfloat16).astype(jnp.float32)
    weight = jnp.exp(CONF_RANGE * jnp.tanh(conf / CONF_RANGE)) * count_row
    for part in range(3):
        cols = slice(part * pixels, (part + 1) * pixels)
        xyz = matmul(head_in, head_ref[:, cols]) + bias_ref[:, cols]
        emit(part, cols, weight, weight * xyz.astype(jnp.bfloat16).astype(jnp.float32))


def view_scratch(tokens, width):
    padded, pairs = round_up(tokens, MXU), width // LANES
    return [
        pltpu.VMEM((padded, width), jnp.bfloat16),
        pltpu.VMEM((pairs, padded, MXU), jnp.bfloat16),
        pltpu.VMEM((tokens, width), jnp.bfloat16),
    ]


def first_kernel(
    scene_size,
    slots,
    offsets_of,
    tokens_hbm,
    qkv_hbm,
    attn_gain_hbm,
    head_gain_hbm,
    bias_hbm,
    list_hbm,
    count_hbm,
    own_ref,
    normed_ref,
    kv_ref,
    gains_ref,
    bias_ref,
    counts_ref,
    q_ref,
    wq_scr,
    list_smem,
    count_smem,
    sems,
):
    tokens, width = own_ref.shape
    head_size = width // HEADS
    rows = q_ref.shape[1] // 2
    first_cols = [slice(start, start + MXU) for start in range(0, width, MXU)]
    plan = [
        (tokens_hbm.at[0], own_ref),
        (attn_gain_hbm, gains_ref.at[0]),
        *((qkv_hbm.at[:, cols], wq_scr.at[:, cols]) for cols in first_cols),
        (list_hbm, list_smem),
        (count_hbm, count_smem),
        (head_gain_hbm, gains_ref.at[1]),
        (bias_hbm, bias_ref.at[0]),
        (qkv_hbm.at[:, width : 2 * width], kv_ref.at[:, :width]),
        (qkv_hbm.at[:, 2 * width :], kv_ref.at[:, width:]),
    ]
    copies = [pltpu.make_async_copy(source, target, sems.at[at]) for at, (source, target) in enumerate(plan)]
    for copy in copies:
        copy.start()
    low_head = lax.broadcasted_iota(jnp.int32, (1, LANES), 1) < head_size
    block = head_block(head_size)
    tail = tokens // 16 * 16
    for half in range(2):
        q_ref[:, half * rows + tail : (half + 1) * rows, :] = jnp.zeros((q_ref.shape[0], rows - tail, LANES), jnp.bfloat16)
    for copy in copies[:2]:
        copy.wait()
    normed_ref[...] = layer_norm(own_ref[...].astype(jnp.float32), gains_ref[0:1, :]).astype(jnp.bfloat16)
    normed = normed_ref[...]
    for at, cols in enumerate(first_cols):
        copies[2 + at].wait()
        unit = head_unit(matmul(normed, wq_scr[:, cols]), block)
        for half in range(MXU // LANES):
            pair = cols.start // LANES + half
            piece = unit[:, half * LANES : (half + 1) * LANES]
            zero = jnp.zeros_like(piece)
            q_ref[pair, :tokens, :] = jnp.where(low_head, piece, zero)
            q_ref[pair, rows : rows + tokens, :] = jnp.where(low_head, zero, piece)
    for copy in copies[2 + len(first_cols) :]:
        copy.wait()
    position = lax.axis_index("scene")
    for at, offset in enumerate(offsets_of(position)):
        partner = lax.rem(position + offset + scene_size, scene_size)
        count = multiplicity(list_smem, count_smem, position, partner, slots).astype(jnp.float32)
        counts_ref[at] = jnp.full(counts_ref.shape[1:], count, jnp.float32)


def is_live(counts_ref, at):
    return jnp.max(counts_ref[at]) > 0


def mate_kernel(gains_ref, counts_ref, q_ref, kv_ref, partner_ref, att_ref, keys_scr, vals_scr):
    position = lax.axis_index("scene")

    @pl.when(jnp.logical_or(position >= 2, jnp.logical_and(position == 1, is_live(counts_ref, 0))))
    def _():
        normed = layer_norm(partner_ref[...].astype(jnp.float32), gains_ref[0:1, :]).astype(jnp.bfloat16)
        attend(normed, q_ref, kv_ref, keys_scr, vals_scr, att_ref)


def mate_maps_kernel(own_ref, gains_ref, bias_ref, counts_ref, q_ref, kv_ref, out_ref, head_ref, partner_ref, *refs):
    _, sums_ref, weights_ref, att_ref, keys_scr, vals_scr = refs
    position = lax.axis_index("scene")
    live = is_live(counts_ref, 0)
    runs = jnp.logical_or(position >= 2, live)

    def emit(part, cols, weight, weighted):
        sums_ref[:, cols] = weighted
        if part == 0:
            weights_ref[...] = weight

    @pl.when(jnp.logical_and(position == 0, live))
    def _():
        normed = layer_norm(partner_ref[...].astype(jnp.float32), gains_ref[0:1, :]).astype(jnp.bfloat16)
        attend(normed, q_ref, kv_ref, keys_scr, vals_scr, att_ref)

    @pl.when(runs)
    def _():
        finish(att_ref[...], counts_ref[0, 0:1, 0:1], own_ref, out_ref, head_ref, gains_ref, bias_ref, emit)

    @pl.when(jnp.logical_not(runs))
    def _():
        sums_ref[...] = jnp.zeros_like(sums_ref)
        weights_ref[...] = jnp.zeros_like(weights_ref)


def view_kernel(at, own_ref, gains_ref, bias_ref, counts_ref, q_ref, kv_ref, out_ref, head_ref, partner_ref, *refs):
    sums_in, weights_in, sums_ref, weights_ref, keys_scr, vals_scr, att_scr = refs

    def emit(part, cols, weight, weighted):
        sums_ref[:, cols] = sums_in[:, cols] + weighted
        if part == 2:
            weights_ref[...] = weights_in[...] + weight

    @pl.when(is_live(counts_ref, at))
    def _():
        normed = layer_norm(partner_ref[...].astype(jnp.float32), gains_ref[0:1, :]).astype(jnp.bfloat16)
        attend(normed, q_ref, kv_ref, keys_scr, vals_scr, att_scr)
        finish(att_scr[...], counts_ref[at, 0:1, 0:1], own_ref, out_ref, head_ref, gains_ref, bias_ref, emit)


def last_kernel(at, own_ref, gains_ref, bias_ref, counts_ref, q_ref, kv_ref, out_ref, head_ref, normed_ref, *refs):
    sums_in, weights_in, joined_hbm, keys_scr, vals_scr, att_scr, joined_scr, sem = refs

    def store(cols, ratio):
        lines = sums_in.shape[1] // LANES
        for line in range(ratio.shape[1] // LANES):
            rows = pl.ds(cols.start // LANES + line, ratio.shape[0], stride=lines)
            joined_scr[rows, :] = ratio[:, line * LANES : (line + 1) * LANES]

    def emit(part, cols, weight, weighted):
        store(cols, (sums_in[:, cols] + weighted) / (weights_in[...] + weight))

    live = is_live(counts_ref, at)

    @pl.when(live)
    def _():
        attend(normed_ref[...], q_ref, kv_ref, keys_scr, vals_scr, att_scr)
        finish(att_scr[...], counts_ref[at, 0:1, 0:1], own_ref, out_ref, head_ref, gains_ref, bias_ref, emit)

    @pl.when(jnp.logical_not(live))
    def _():
        pixels = weights_in.shape[1]
        for part in range(3):
            cols = slice(part * pixels, (part + 1) * pixels)
            store(cols, sums_in[:, cols] / weights_in[...])

    copy = pltpu.make_async_copy(joined_scr, joined_hbm, sem)
    copy.start()
    copy.wait()


def per_device(
    tokens, qkv_weight, out_weight, attn_gain, head_gain, head_weight, head_bias, pair_list, pair_count
):
    scene_size = lax.axis_size("scene")
    _, token_count, width = tokens.shape
    slots = pair_list.shape[0] // scene_size
    columns = head_weight.shape[1]
    pixels = columns // 4
    f32, bf16 = jnp.float32, jnp.bfloat16
    own = tokens[0]

    def moved(value, target_of):
        return lax.ppermute(value, "scene", [(s, target_of(s) % scene_size) for s in range(scene_size)])

    def mate_of(s):
        return s ^ 1

    def offsets_of(position):
        to_mate = 1 - 2 * lax.rem(position, 2)
        return (to_mate, -to_mate, 2 * to_mate, -2 * to_mate)

    sums = jax.ShapeDtypeStruct((token_count, 3 * pixels), f32)
    weights = jax.ShapeDtypeStruct((token_count, pixels), f32)
    params = pltpu.CompilerParams(vmem_limit_bytes=24 * 2**20)
    cost = pl.CostEstimate(flops=4 * token_count * width * width * 2, bytes_accessed=2**20, transcendentals=0)

    alpha = moved(own, lambda s: s + 1 if s % 2 else s - 1)
    mate = moved(own, mate_of)
    first_shapes = (
        jax.ShapeDtypeStruct((token_count, width), bf16),
        jax.ShapeDtypeStruct((token_count, width), bf16),
        jax.ShapeDtypeStruct((width, 2 * width), bf16),
        jax.ShapeDtypeStruct((2, width), f32),
        jax.ShapeDtypeStruct((1, columns), f32),
        jax.ShapeDtypeStruct((4, 8, LANES), f32),
        jax.ShapeDtypeStruct((width // LANES, 2 * round_up(token_count, 16), LANES), bf16),
    )
    own_vmem, normed, kv_vmem, gains, bias, counts, queries = pl.pallas_call(
        functools.partial(first_kernel, scene_size, slots, offsets_of),
        out_shape=first_shapes,
        in_specs=[HBM_SPEC] * 7,
        out_specs=tuple(VMEM_SPEC for _ in first_shapes),
        scratch_shapes=[
            pltpu.VMEM((width, width), bf16),
            pltpu.SMEM((2, pair_list.shape[0]), jnp.int32),
            pltpu.SMEM(pair_count.shape, jnp.int32),
            pltpu.SemaphoreType.DMA((8 + width // MXU,)),
        ],
        compiler_params=params,
        cost_estimate=cost,
        name="load_queries",
    )(
        in_hbm(tokens),
        *(in_hbm(value) for value in (qkv_weight, attn_gain, head_gain, head_bias)),
        in_hbm(pair_list.T),
        in_hbm(pair_count),
    )

    def kernel(body, operands, in_specs, out_shape, out_spec, scratch, aliases={}):
        return pl.pallas_call(
            body,
            out_shape=out_shape,
            in_specs=in_specs,
            out_specs=[out_spec] * len(out_shape),
            scratch_shapes=scratch,
            input_output_aliases=aliases,
            compiler_params=params,
            cost_estimate=cost,
        )(*operands)

    scratch = view_scratch(token_count, width)
    (attended,) = kernel(
        mate_kernel,
        (gains, counts, queries, kv_vmem, mate),
        [VMEM_SPEC] * 5,
        [jax.ShapeDtypeStruct((token_count, width), bf16)],
        VMEM_SPEC,
        scratch[:2],
    )
    normed, attended = lax.optimization_barrier((normed, attended))
    beta = moved(normed, lambda s: s - 2 if s % 2 else s + 2)
    common = (own_vmem, gains, bias, counts, queries, kv_vmem, out_weight, head_weight)
    *totals, _ = kernel(
        mate_maps_kernel,
        (*common, mate, attended),
        [VMEM_SPEC] * 10,
        (sums, weights, jax.ShapeDtypeStruct((token_count, width), bf16)),
        VMEM_SPEC,
        scratch[:2],
        {9: 2},
    )
    alpha, *totals = lax.optimization_barrier((alpha, *totals))
    swapped = moved(alpha, mate_of)
    for at, partner in ((1, alpha), (2, swapped)):
        totals = kernel(
            functools.partial(view_kernel, at),
            (*common, partner, *totals),
            [VMEM_SPEC] * 11,
            (sums, weights),
            VMEM_SPEC,
            scratch,
            {9: 0, 10: 1},
        )
    joined_shape = jax.ShapeDtypeStruct((token_count * 3 * pixels // LANES, LANES), f32)
    (joined,) = kernel(
        functools.partial(last_kernel, 3),
        (*common, beta, *totals),
        [VMEM_SPEC] * 11,
        (joined_shape,),
        HBM_SPEC,
        scratch + [pltpu.VMEM(joined_shape.shape, f32), pltpu.SemaphoreType.DMA],
    )
    return joined.reshape(1, token_count, 3 * pixels)


def solution(mesh):
    return jax.shard_map(
        per_device,
        mesh=mesh,
        in_specs=(
            P(("groups", "scene"), None, None),
            P(),
            P(),
            P(),
            P(),
            P(),
            P(),
            P("groups", None),
            P("groups"),
        ),
        out_specs=P(("groups", "scene"), None, None),
        check_vma=False,
    )
```

```python
import functools

import jax
import jax.numpy as jnp
from jax import lax
from jax.experimental import pallas as pl
from jax.experimental.pallas import tpu as pltpu
from jax.sharding import PartitionSpec as P


HEADS = 12
TEMPER = 16.0
CONF_RANGE = 4.0
EPSILON = 1e-06
LANES = 128
MXU = 256

VMEM_SPEC = pl.BlockSpec(memory_space=pltpu.VMEM)
HBM_SPEC = pl.BlockSpec(memory_space=pltpu.HBM)


def in_hbm(value):
    return pltpu.with_memory_space_constraint(value, pltpu.HBM)


def round_up(value, step):
    return -(-value // step) * step


def layer_norm(values, gain_row):
    centred = values - jnp.mean(values, axis=-1, keepdims=True)
    spread = jnp.mean(centred * centred, axis=-1, keepdims=True)
    return centred * lax.rsqrt(spread + EPSILON) * gain_row


def matmul(left, right):
    return jnp.dot(left, right, preferred_element_type=jnp.float32)


def head_block(head_size):
    rows = lax.broadcasted_iota(jnp.int32, (MXU, MXU), 0) // head_size
    cols = lax.broadcasted_iota(jnp.int32, (MXU, MXU), 1) // head_size
    return jnp.where(rows == cols, 1.0 / head_size, 0.0).astype(jnp.bfloat16)


def head_unit(mixed, block):
    energy = matmul((mixed * mixed).astype(jnp.bfloat16), block)
    return (mixed * lax.rsqrt(energy + EPSILON)).astype(jnp.bfloat16)


def multiplicity(pair_list, pair_count, own, partner, slots):
    count = jnp.int32(0)
    for slot in range(slots):
        for first, second in ((own, partner), (partner, own)):
            live = slot < pair_count[first]
            hit = pair_list[1, first * slots + slot] == second
            count = count + jnp.where(jnp.logical_and(live, hit), 1, 0)
    return count


def attend(normed, q_ref, kv_ref, keys_scr, vals_scr, att_ref):
    tokens, width = normed.shape
    head_size = width // HEADS
    rows = q_ref.shape[1] // 2
    padded = keys_scr.shape[0]
    pairs = width // LANES
    low_head = lax.broadcasted_iota(jnp.int32, (1, LANES), 1) < head_size
    block = head_block(head_size)

    tail = tokens // 16 * 16
    keys_scr[tail:, :] = jnp.zeros((padded - tail, width), jnp.bfloat16)
    row = lax.broadcasted_iota(jnp.int32, (padded, LANES), 0)
    ones = jnp.where(row < tokens, 1.0, 0.0).astype(jnp.bfloat16)
    for pair in range(pairs):
        vals_scr[pair, tail:, :LANES] = jnp.zeros((padded - tail, LANES), jnp.bfloat16)
        vals_scr[pair, :, LANES:] = ones

    for start in range(0, width, MXU):
        keys_scr[:tokens, start : start + MXU] = head_unit(matmul(normed, kv_ref[:, start : start + MXU]), block)
        value = matmul(normed, kv_ref[:, width + start : width + start + MXU]).astype(jnp.bfloat16)
        for half in range(MXU // LANES):
            vals_scr[start // LANES + half, :tokens, :LANES] = value[:, half * LANES : (half + 1) * LANES]
    for pair in range(pairs):
        scores = lax.dot_general(
            q_ref[pair],
            keys_scr[:, pair * LANES : (pair + 1) * LANES],
            (((1,), (1,)), ((), ())),
            preferred_element_type=jnp.float32,
        )
        exponent = jnp.exp(scores * (TEMPER / head_size)).astype(jnp.bfloat16)
        mixed = matmul(exponent, vals_scr[pair])
        top = jnp.where(low_head, mixed[:tokens, :LANES], mixed[rows : rows + tokens, :LANES])
        norm = jnp.where(low_head, mixed[:tokens, LANES:], mixed[rows : rows + tokens, LANES:])
        att_ref[:, pair * LANES : (pair + 1) * LANES] = (top / norm).astype(jnp.bfloat16)


def finish(attended, count_row, own_ref, out_ref, head_ref, gains_ref, bias_ref, emit):
    pixels = head_ref.shape[1] // 4
    mixed = own_ref[...].astype(jnp.float32) + matmul(attended, out_ref[...])
    head_in = layer_norm(mixed, gains_ref[1:2, :]).astype(jnp.bfloat16)
    conf = matmul(head_in, head_ref[:, 3 * pixels :]) + bias_ref[:, 3 * pixels :]
    conf = conf.astype(jnp.bfloat16).astype(jnp.float32)
    weight = jnp.exp(CONF_RANGE * jnp.tanh(conf / CONF_RANGE)) * count_row
    for part in range(3):
        cols = slice(part * pixels, (part + 1) * pixels)
        xyz = matmul(head_in, head_ref[:, cols]) + bias_ref[:, cols]
        emit(part, cols, weight, weight * xyz.astype(jnp.bfloat16).astype(jnp.float32))


def view_scratch(tokens, width):
    padded, pairs = round_up(tokens, MXU), width // LANES
    return [
        pltpu.VMEM((padded, width), jnp.bfloat16),
        pltpu.VMEM((pairs, padded, MXU), jnp.bfloat16),
        pltpu.VMEM((tokens, width), jnp.bfloat16),
    ]


def first_kernel(
    scene_size,
    slots,
    offsets_of,
    tokens_hbm,
    qkv_hbm,
    attn_gain_hbm,
    head_gain_hbm,
    bias_hbm,
    list_hbm,
    count_hbm,
    own_ref,
    normed_ref,
    kv_ref,
    gains_ref,
    bias_ref,
    counts_ref,
    q_ref,
    wq_scr,
    list_smem,
    count_smem,
    sems,
):
    tokens, width = own_ref.shape
    head_size = width // HEADS
    rows = q_ref.shape[1] // 2
    first_cols = [slice(start, start + MXU) for start in range(0, width, MXU)]
    plan = [
        (tokens_hbm.at[0], own_ref),
        (attn_gain_hbm, gains_ref.at[0]),
        *((qkv_hbm.at[:, cols], wq_scr.at[:, cols]) for cols in first_cols),
        (list_hbm, list_smem),
        (count_hbm, count_smem),
        (head_gain_hbm, gains_ref.at[1]),
        (bias_hbm, bias_ref.at[0]),
        (qkv_hbm.at[:, width : 2 * width], kv_ref.at[:, :width]),
        (qkv_hbm.at[:, 2 * width :], kv_ref.at[:, width:]),
    ]
    copies = [pltpu.make_async_copy(source, target, sems.at[at]) for at, (source, target) in enumerate(plan)]
    for copy in copies:
        copy.start()
    low_head = lax.broadcasted_iota(jnp.int32, (1, LANES), 1) < head_size
    block = head_block(head_size)
    tail = tokens // 16 * 16
    for half in range(2):
        q_ref[:, half * rows + tail : (half + 1) * rows, :] = jnp.zeros((q_ref.shape[0], rows - tail, LANES), jnp.bfloat16)
    for copy in copies[:2]:
        copy.wait()
    normed_ref[...] = layer_norm(own_ref[...].astype(jnp.float32), gains_ref[0:1, :]).astype(jnp.bfloat16)
    normed = normed_ref[...]
    for at, cols in enumerate(first_cols):
        copies[2 + at].wait()
        unit = head_unit(matmul(normed, wq_scr[:, cols]), block)
        for half in range(MXU // LANES):
            pair = cols.start // LANES + half
            piece = unit[:, half * LANES : (half + 1) * LANES]
            zero = jnp.zeros_like(piece)
            q_ref[pair, :tokens, :] = jnp.where(low_head, piece, zero)
            q_ref[pair, rows : rows + tokens, :] = jnp.where(low_head, zero, piece)
    for copy in copies[2 + len(first_cols) :]:
        copy.wait()
    position = lax.axis_index("scene")
    for at, offset in enumerate(offsets_of(position)):
        partner = lax.rem(position + offset + scene_size, scene_size)
        count = multiplicity(list_smem, count_smem, position, partner, slots).astype(jnp.float32)
        counts_ref[at] = jnp.full(counts_ref.shape[1:], count, jnp.float32)


def is_live(counts_ref, at):
    return jnp.max(counts_ref[at, 0:1, 0:1]) > 0


def mate_runs(counts_ref):
    return jnp.logical_or(is_live(counts_ref, 0), lax.axis_index("scene") >= 2)


def mate_kernel(gains_ref, counts_ref, q_ref, kv_ref, partner_ref, att_ref, keys_scr, vals_scr):
    @pl.when(mate_runs(counts_ref))
    def _():
        normed = layer_norm(partner_ref[...].astype(jnp.float32), gains_ref[0:1, :]).astype(jnp.bfloat16)
        attend(normed, q_ref, kv_ref, keys_scr, vals_scr, att_ref)


def mate_maps_kernel(own_ref, gains_ref, bias_ref, counts_ref, att_ref, out_ref, head_ref, sums_ref, weights_ref):
    def emit(part, cols, weight, weighted):
        sums_ref[:, cols] = weighted
        if part == 0:
            weights_ref[...] = weight

    runs = mate_runs(counts_ref)

    @pl.when(runs)
    def _():
        finish(att_ref[...], counts_ref[0, 0:1, 0:1], own_ref, out_ref, head_ref, gains_ref, bias_ref, emit)

    @pl.when(jnp.logical_not(runs))
    def _():
        sums_ref[...] = jnp.zeros_like(sums_ref)
        weights_ref[...] = jnp.zeros_like(weights_ref)


def view_kernel(at, own_ref, gains_ref, bias_ref, counts_ref, q_ref, kv_ref, out_ref, head_ref, partner_ref, *refs):
    sums_in, weights_in, sums_ref, weights_ref, keys_scr, vals_scr, att_scr = refs

    def emit(part, cols, weight, weighted):
        sums_ref[:, cols] = sums_in[:, cols] + weighted
        if part == 2:
            weights_ref[...] = weights_in[...] + weight

    @pl.when(is_live(counts_ref, at))
    def _():
        normed = layer_norm(partner_ref[...].astype(jnp.float32), gains_ref[0:1, :]).astype(jnp.bfloat16)
        attend(normed, q_ref, kv_ref, keys_scr, vals_scr, att_scr)
        finish(att_scr[...], counts_ref[at, 0:1, 0:1], own_ref, out_ref, head_ref, gains_ref, bias_ref, emit)


def last_kernel(at, own_ref, gains_ref, bias_ref, counts_ref, q_ref, kv_ref, out_ref, head_ref, normed_ref, *refs):
    sums_in, weights_in, joined_hbm, keys_scr, vals_scr, att_scr, joined_scr, sem = refs

    def store(cols, ratio):
        lines = sums_in.shape[1] // LANES
        for line in range(ratio.shape[1] // LANES):
            rows = pl.ds(cols.start // LANES + line, ratio.shape[0], stride=lines)
            joined_scr[rows, :] = ratio[:, line * LANES : (line + 1) * LANES]

    def emit(part, cols, weight, weighted):
        store(cols, (sums_in[:, cols] + weighted) / (weights_in[...] + weight))

    live = is_live(counts_ref, at)

    @pl.when(live)
    def _():
        attend(normed_ref[...], q_ref, kv_ref, keys_scr, vals_scr, att_scr)
        finish(att_scr[...], counts_ref[at, 0:1, 0:1], own_ref, out_ref, head_ref, gains_ref, bias_ref, emit)

    @pl.when(jnp.logical_not(live))
    def _():
        pixels = weights_in.shape[1]
        for part in range(3):
            cols = slice(part * pixels, (part + 1) * pixels)
            store(cols, sums_in[:, cols] / weights_in[...])

    copy = pltpu.make_async_copy(joined_scr, joined_hbm, sem)
    copy.start()
    copy.wait()


def per_device(
    tokens, qkv_weight, out_weight, attn_gain, head_gain, head_weight, head_bias, pair_list, pair_count
):
    scene_size = lax.axis_size("scene")
    _, token_count, width = tokens.shape
    slots = pair_list.shape[0] // scene_size
    columns = head_weight.shape[1]
    pixels = columns // 4
    f32, bf16 = jnp.float32, jnp.bfloat16
    own = tokens[0]

    def moved(value, target_of):
        return lax.ppermute(value, "scene", [(s, target_of(s) % scene_size) for s in range(scene_size)])

    def mate_of(s):
        return s ^ 1

    def offsets_of(position):
        to_mate = 1 - 2 * lax.rem(position, 2)
        return (to_mate, -to_mate, 2 * to_mate, -2 * to_mate)

    sums = jax.ShapeDtypeStruct((token_count, 3 * pixels), f32)
    weights = jax.ShapeDtypeStruct((token_count, pixels), f32)
    params = pltpu.CompilerParams(vmem_limit_bytes=24 * 2**20)
    cost = pl.CostEstimate(flops=4 * token_count * width * width * 2, bytes_accessed=2**20, transcendentals=0)

    alpha = moved(own, lambda s: s + 1 if s % 2 else s - 1)
    mate = moved(own, mate_of)
    first_shapes = (
        jax.ShapeDtypeStruct((token_count, width), bf16),
        jax.ShapeDtypeStruct((token_count, width), bf16),
        jax.ShapeDtypeStruct((width, 2 * width), bf16),
        jax.ShapeDtypeStruct((2, width), f32),
        jax.ShapeDtypeStruct((1, columns), f32),
        jax.ShapeDtypeStruct((4, 8, LANES), f32),
        jax.ShapeDtypeStruct((width // LANES, 2 * round_up(token_count, 16), LANES), bf16),
    )
    own_vmem, normed, kv_vmem, gains, bias, counts, queries = pl.pallas_call(
        functools.partial(first_kernel, scene_size, slots, offsets_of),
        out_shape=first_shapes,
        in_specs=[HBM_SPEC] * 7,
        out_specs=tuple(VMEM_SPEC for _ in first_shapes),
        scratch_shapes=[
            pltpu.VMEM((width, width), bf16),
            pltpu.SMEM((2, pair_list.shape[0]), jnp.int32),
            pltpu.SMEM(pair_count.shape, jnp.int32),
            pltpu.SemaphoreType.DMA((8 + width // MXU,)),
        ],
        compiler_params=params,
        cost_estimate=cost,
        name="load_queries",
    )(
        in_hbm(tokens),
        *(in_hbm(value) for value in (qkv_weight, attn_gain, head_gain, head_bias)),
        in_hbm(pair_list.T),
        in_hbm(pair_count),
    )

    def kernel(body, operands, in_specs, out_shape, out_spec, scratch, aliases={}):
        return pl.pallas_call(
            body,
            out_shape=out_shape,
            in_specs=in_specs,
            out_specs=[out_spec] * len(out_shape),
            scratch_shapes=scratch,
            input_output_aliases=aliases,
            compiler_params=params,
            cost_estimate=cost,
        )(*operands)

    scratch = view_scratch(token_count, width)
    (attended,) = kernel(
        mate_kernel,
        (gains, counts, queries, kv_vmem, mate),
        [VMEM_SPEC] * 5,
        [jax.ShapeDtypeStruct((token_count, width), bf16)],
        VMEM_SPEC,
        scratch[:2],
    )
    normed, attended = lax.optimization_barrier((normed, attended))
    beta = moved(normed, lambda s: s - 2 if s % 2 else s + 2)
    totals = kernel(
        mate_maps_kernel,
        (own_vmem, gains, bias, counts, attended, out_weight, head_weight),
        [VMEM_SPEC] * 7,
        (sums, weights),
        VMEM_SPEC,
        [],
    )
    alpha, *totals = lax.optimization_barrier((alpha, *totals))
    swapped = moved(alpha, mate_of)
    common = (own_vmem, gains, bias, counts, queries, kv_vmem, out_weight, head_weight)
    for at, partner in ((1, alpha), (2, swapped)):
        totals = kernel(
            functools.partial(view_kernel, at),
            (*common, partner, *totals),
            [VMEM_SPEC] * 11,
            (sums, weights),
            VMEM_SPEC,
            scratch,
            {9: 0, 10: 1},
        )
    joined_shape = jax.ShapeDtypeStruct((token_count * 3 * pixels // LANES, LANES), f32)
    (joined,) = kernel(
        functools.partial(last_kernel, 3),
        (*common, beta, *totals),
        [VMEM_SPEC] * 11,
        (joined_shape,),
        HBM_SPEC,
        scratch + [pltpu.VMEM(joined_shape.shape, f32), pltpu.SemaphoreType.DMA],
    )
    return joined.reshape(1, token_count, 3 * pixels)


def solution(mesh):
    return jax.shard_map(
        per_device,
        mesh=mesh,
        in_specs=(
            P(("groups", "scene"), None, None),
            P(),
            P(),
            P(),
            P(),
            P(),
            P(),
            P("groups", None),
            P("groups"),
        ),
        out_specs=P(("groups", "scene"), None, None),
        check_vma=False,
    )
```
